32 devices in a mesh: sect: 2 (over core), lang: 4 (over z), mp: 4 (over y, x).
Axes of the slice: x: 2, y: 2, z: 4, core: 2. Of those that a mesh axis runs over, the one named last changes fastest.
Arguments:
- memory: bfloat16 [4, 2, 128, 4096], P('lang', None, None, ('sect', 'mp')), may hold values from -6 to 6
- queries: bfloat16 [4, 4, 128, 3072], P('lang', 'sect', None, 'mp'), may hold values from -6 to 6
- out_grad: bfloat16 [4, 4, 128, 3072], P('lang', 'sect', None, 'mp'), may hold values from -6 to 6
- key_weight: bfloat16 [4, 4096, 3072], P('lang', None, 'mp'), may hold values from -0.09375 to 0.09375
- value_weight: bfloat16 [4, 4096, 3072], P('lang', None, 'mp'), may hold values from -0.09375 to 0.09375
- lang_rows: int32 [4, 4], P('lang'), may hold values from 0 to 128, as said below
- group_of_lang: int32 [4], replicated, may hold values from 0 to 3, each once
- src_len: int32 [4, 2], P('lang'), may hold values from 16 to 128
Outputs:
- mem_grad: bfloat16 [4, 2, 128, 4096], P('lang', None, None, ('sect', 'mp'))
The draws below stay inside these ranges and needn't reach their ends.
Inputs may be any that keep to these rules, and one draw needn't show every extreme that they name: `lang_rows`: each entry is 0 or 128; each row has exactly 2 nonzero entries.
All inputs are finite; a program needn't handle non-finite values.
Results may differ from the reference program's by a relative error of at most 0.013.
Values may be sent and summed in bfloat16 or wider, within the bound.
A program may use at most 128 MiB of HBM per device.

```python
import jax
import jax.numpy as jnp
from jax import lax

D = 4096
HEADS = 24
HD = 128
SRC_LEN = 128
TGT = 128
TARGET_LANGUAGES = 4
BLK_DEV = 2
N_LANG = 4


def draw_lang_rows(key, part):
    key_heavy, key_first, key_noise = jax.random.split(key, 3)
    busiest_language = jax.random.randint(key_heavy, (TARGET_LANGUAGES,), 0, 4)
    leading_language = jax.random.randint(key_first, (), 0, TARGET_LANGUAGES)
    random_noise = jax.random.randint(key_noise, (TARGET_LANGUAGES, TARGET_LANGUAGES), 0, 65536)
    language_index = jnp.arange(TARGET_LANGUAGES, dtype=jnp.int32)
    extra_score = jnp.where(language_index == leading_language, 8 * 65536, 0) + busiest_language * 65536
    score_table = (random_noise + extra_score[None, :]) * TARGET_LANGUAGES + language_index[None, :]
    picked_values, top_index = lax.top_k(score_table, BLK_DEV)
    chosen = jnp.sum((top_index[:, :, None] == language_index[None, None, :]).astype(jnp.int32), axis=1)
    return (chosen * SRC_LEN).astype(jnp.int32)


def draw_src_len(key, part):
    key_base, key_spot = jax.random.split(jax.random.fold_in(key, 7))
    base_len = jax.random.randint(key_base, (TARGET_LANGUAGES, BLK_DEV), SRC_LEN // 8, SRC_LEN + 1)
    spot_index = jax.random.randint(key_spot, (), 0, TARGET_LANGUAGES * BLK_DEV)
    flat_index = jnp.arange(TARGET_LANGUAGES * BLK_DEV, dtype=jnp.int32).reshape(TARGET_LANGUAGES, BLK_DEV)
    return jnp.where(flat_index == spot_index, SRC_LEN, base_len).astype(jnp.int32)


def block_levels(rng, shape, cuts, smallest, largest):
    gain, own = 1.0, jax.random.fold_in(rng, 6)
    for axis_at, blocks in cuts:
        heights = jnp.exp(jax.random.uniform(jax.random.fold_in(own, axis_at), (blocks,), jnp.float32, smallest / len(cuts), largest / len(cuts)))
        gain = gain * jnp.repeat(heights, shape[axis_at] // blocks).reshape([-1 if axis == axis_at else 1 for axis in range(len(shape))])
    return gain


def scatter_about(own_key, extent, spread, limit, cuts=(), held_as=jnp.bfloat16):
    entries = jax.random.normal(own_key, extent, jnp.float32) * spread
    if len(cuts) > 0:
        entries = block_levels(own_key, extent, cuts, -0.22, 0.18) * entries
    return jnp.clip(entries, min=-limit, max=limit).astype(held_as)


def setup_inputs(seed: int = 0) -> dict:
    key_list = jax.random.split(jax.random.key(seed), 9)
    memory = scatter_about(key_list[0], (N_LANG, BLK_DEV, SRC_LEN, D), 1.0, 6.0, ((0, 4), (3, 8)))
    queries = scatter_about(key_list[1], (N_LANG, N_LANG, TGT, HEADS * HD), 1.0, 6.0, ((0, 4), (1, 2), (3, 4)))
    out_grad = scatter_about(key_list[2], (N_LANG, N_LANG, TGT, HEADS * HD), 1.0, 6.0, ((0, 4), (1, 2), (3, 4)))
    key_weight = scatter_about(key_list[3], (N_LANG, D, HEADS * HD), D ** -0.5, 0.09375, ((0, 4), (2, 4)))
    value_weight = scatter_about(key_list[4], (N_LANG, D, HEADS * HD), D ** -0.5, 0.09375, ((0, 4), (2, 4)))
    lang_rows = draw_lang_rows(jax.random.fold_in(key_list[8], 71), 0)
    group_of_lang = jax.random.permutation(key_list[6], TARGET_LANGUAGES).astype(jnp.int32)
    src_len = draw_src_len(jax.random.fold_in(key_list[8], 71), 0)
    return dict(memory=memory, queries=queries, out_grad=out_grad, key_weight=key_weight, value_weight=value_weight, lang_rows=lang_rows, group_of_lang=group_of_lang, src_len=src_len)


def key_grads(key_rows, value_rows, queries, out_grad, lengths, head_dim):
    slots, source, width = key_rows.shape
    target = queries.shape[1]
    heads = width // head_dim
    key_four = key_rows.reshape(slots, source, heads, head_dim).astype(jnp.float32)
    value_four = value_rows.reshape(slots, source, heads, head_dim).astype(jnp.float32)
    query_four = queries.reshape(slots, target, heads, head_dim).astype(jnp.float32)
    grad_four = out_grad.reshape(slots, target, heads, head_dim).astype(jnp.float32)
    scaling = head_dim ** -0.5
    score_table = jnp.einsum("sqhd,skhd->shqk", query_four, key_four) * scaling
    visible = jnp.arange(source, dtype=jnp.int32)[None, :] < lengths[:, None]
    weights = jnp.where(visible[:, None, None, :], jnp.exp(score_table), 0.0)
    probs = weights / jnp.sum(weights, axis=-1, keepdims=True)
    probs_low = probs.astype(jnp.bfloat16)
    grad_probs = jnp.einsum("sqhd,skhd->shqk", grad_four, value_four)
    deltas = jnp.sum(probs * grad_probs, axis=-1, keepdims=True)
    grad_scores = (probs * (grad_probs - deltas) * scaling).astype(jnp.bfloat16)
    grad_keys = jnp.einsum("shqk,sqhd->skhd", grad_scores.astype(jnp.float32), query_four)
    grad_values = jnp.einsum("shqk,sqhd->skhd", probs_low.astype(jnp.float32), grad_four)
    grad_keys = grad_keys.astype(jnp.bfloat16).reshape(slots, source, width)
    grad_values = grad_values.astype(jnp.bfloat16).reshape(slots, source, width)
    return grad_keys, grad_values


def reference(memory, queries, out_grad, key_weight, value_weight, lang_rows, group_of_lang, src_len):
    shards = memory.shape[0]
    blocks = memory.shape[1]
    is_live = (lang_rows > 0).astype(jnp.int32)
    ranking = jnp.cumsum(is_live, axis=1) - 1
    block_index = jnp.arange(blocks, dtype=jnp.int32)
    chosen = (is_live[:, None, :] > 0) & (ranking[:, None, :] == block_index[None, :, None])
    language_index = jnp.arange(lang_rows.shape[1], dtype=jnp.int32)
    block_lang = jnp.sum(jnp.where(chosen, language_index[None, None, :], 0), axis=2).astype(jnp.int32)
    block_group = group_of_lang[block_lang].astype(jnp.int32)

    def one_block(flat):
        shard = flat // blocks
        within = flat % blocks
        group = block_group[shard, within]
        panel = memory[shard, within]
        key_rows = jnp.dot(panel, key_weight[group], preferred_element_type=jnp.float32).astype(jnp.bfloat16)
        value_rows = jnp.dot(panel, value_weight[group], preferred_element_type=jnp.float32).astype(jnp.bfloat16)
        grad_keys, grad_values = key_grads(key_rows[None], value_rows[None], queries[group, shard][None], out_grad[group, shard][None], src_len[shard, within][None], HD)
        term = jnp.dot(grad_keys[0], key_weight[group].T, preferred_element_type=jnp.float32)
        term = term + jnp.dot(grad_values[0], value_weight[group].T, preferred_element_type=jnp.float32)
        return term.astype(jnp.bfloat16)

    result = lax.map(one_block, jnp.arange(shards * blocks, dtype=jnp.int32))
    return result.reshape(memory.shape)
```

```python
import functools

import jax
import jax.numpy as jnp
from jax import lax
from jax.experimental import pallas as pl
from jax.experimental.pallas import tpu as pltpu
from jax.sharding import PartitionSpec as P

HD = 128
LANES = 256
MESH = pl.DeviceIdType.MESH
NT = (((1,), (1,)), ((), ()))


def kernel(
    dims,
    lang_rows,
    group_of_lang,
    src_len,
    memory_hbm,
    queries_hbm,
    grads_hbm,
    key_hbm,
    value_hbm,
    out,
    weights,
    turned,
    memory,
    query_v,
    grad_v,
    outgoing,
    out_len,
    got_len,
    rows,
    acc,
    row_grads,
    part,
    own,
    inbox,
    reduced,
    arrived,
    load_sem,
    z_send,
    z_len_send,
    len_recv,
    rows_recv,
    mp_send,
    part_send,
    part_recv,
    back_send,
    back_recv,
):
    sectors, groups, quarters, half, blocks, source, eighth, width, heads_w = dims
    ms, ml, mq = lax.axis_index("sect"), lax.axis_index("lang"), lax.axis_index("mp")
    languages = lang_rows.shape[1]

    loads = [
        pltpu.make_async_copy(key_hbm.at[0], weights.at[:, pl.ds(0, heads_w)], load_sem.at[0]),
        pltpu.make_async_copy(
            value_hbm.at[0], weights.at[:, pl.ds(heads_w, heads_w)], load_sem.at[1]
        ),
        pltpu.make_async_copy(queries_hbm.at[0], query_v, load_sem.at[2]),
        pltpu.make_async_copy(grads_hbm.at[0], grad_v, load_sem.at[3]),
    ]

    fetch = pltpu.make_async_copy(memory_hbm, memory, load_sem.at[4])
    fetch.start()
    barrier = pltpu.get_barrier_semaphore()
    for ds in range(sectors):
        for dl in range(groups):
            if ds or dl:
                peer = (lax.rem(ms + ds, sectors), lax.rem(ml + dl, groups), mq)
                pl.semaphore_signal(barrier, inc=1, device_id=peer, device_id_type=MESH)
    for dq in range(1, quarters):
        peer = (ms, ml, lax.rem(mq + dq, quarters))
        pl.semaphore_signal(barrier, inc=1, device_id=peer, device_id_type=MESH)
    for load in loads:
        load.start()

    live, rank, count = [], [], 0
    for c in range(languages):
        live.append((lang_rows[0, c] > 0).astype(jnp.int32))
        rank.append(count)
        count = count + live[c]
    home = lax.div(ml, half)
    slot = lax.rem(ml, half)
    at_home = home == ms
    fetch.wait()
    for g in range(groups):
        index, routed = 0, 0
        for c in range(languages):
            hit = jnp.where(group_of_lang[c] == g, live[c], 0)
            index = index + hit * rank[c]
            routed = routed + hit
        outgoing[g] = memory[0, index]
        length = jnp.maximum(jnp.where(routed > 0, src_len[0, index], 1), 1)
        out_len[g] = jnp.full(out_len.shape[1:], length, jnp.int32)

    pl.semaphore_wait(barrier, sectors * groups - 1 + quarters - 1)

    side = jnp.where(ml < groups - 1 - ml, 1, -1)
    edge = jnp.minimum(ml, groups - 1 - ml)

    def nth(i):
        near = (i + 1) // 2 if i % 2 else -(i // 2)
        return ml + side * jnp.where(i <= 2 * edge, near, i - edge)

    def z_copy(i):
        g = nth(i)
        data = pltpu.make_async_remote_copy(
            src_ref=outgoing.at[g],
            dst_ref=rows.at[ms, mq, slot],
            send_sem=z_send.at[g],
            recv_sem=rows_recv.at[ms, mq, slot],
            device_id=(home, g, mq),
            device_id_type=MESH,
        )
        lens = pltpu.make_async_remote_copy(
            src_ref=out_len.at[g],
            dst_ref=got_len.at[slot, ms],
            send_sem=z_len_send.at[g],
            recv_sem=len_recv.at[slot, ms],
            device_id=(home, g, mq),
            device_id_type=MESH,
        )
        return data, lens

    def local_in():
        return (
            pltpu.make_async_copy(
                outgoing.at[ml], rows.at[ms, mq, slot], rows_recv.at[ms, mq, slot]
            ),
            pltpu.make_async_copy(
                out_len.at[ml], got_len.at[slot, ms], len_recv.at[slot, ms]
            ),
        )

    @pl.when(at_home)
    def _():
        for copy in local_in():
            copy.start()

    @pl.when(jnp.logical_not(at_home))
    def _():
        for copy in z_copy(0):
            copy.start()

    for i in range(1, groups):
        for copy in z_copy(i):
            copy.start()

    relay = quarters == 4

    def peer(dq):
        if not relay:
            return lax.rem(mq + dq, quarters)
        near = mq + 1 - 2 * lax.rem(mq, 2)
        far = mq + 2 - 4 * lax.div(mq, 2)
        if isinstance(dq, int):
            return (mq, near, far, 3 - mq)[dq]
        return jnp.where(dq == 0, mq, jnp.where(dq == 1, near, jnp.where(dq == 2, far, 3 - mq)))

    def first_axis(s):
        return 1 + s % 2 if isinstance(s, int) else 1 + lax.rem(s, 2)

    def landed(s, q, ls):
        view = rows.at[s, q, ls]
        pltpu.make_async_copy(view, view, rows_recv.at[s, q, ls]).wait()

    def mp_copy(s, ls, dq):
        return pltpu.make_async_remote_copy(
            src_ref=rows.at[s, mq, ls],
            dst_ref=rows.at[s, mq, ls],
            send_sem=mp_send.at[dq - 1, s, ls],
            recv_sem=rows_recv.at[s, mq, ls],
            device_id=(ms, ml, peer(dq)),
            device_id_type=MESH,
        )

    def relay_copy(s, ls):
        q = peer(3 - first_axis(s))
        return pltpu.make_async_remote_copy(
            src_ref=rows.at[s, q, ls],
            dst_ref=rows.at[s, q, ls],
            send_sem=mp_send.at[2, s, ls],
            recv_sem=rows_recv.at[s, q, ls],
            device_id=(ms, ml, peer(first_axis(s))),
            device_id_type=MESH,
        )

    nearest = jnp.clip(ml - ms * half, 0, half - 1)

    def slot_of(k):
        return lax.rem(nearest + k, half)

    spread = (2, 1) if relay else tuple(range(quarters - 1, 0, -1))

    def gather(ls, s):
        landed(s, mq, ls)
        for dq in spread:
            mp_copy(s, ls, dq).start()

    def pass_on(ls, s):
        if relay:
            landed(s, peer(3 - first_axis(s)), ls)
            relay_copy(s, ls).start()

    def rows_of(s, q):
        return pl.ds(pl.multiple_of((s * quarters + q) * eighth, eighth), eighth)

    def turn(first, last):
        def step(i, carry):
            at = pl.ds(pl.multiple_of(i * eighth, eighth), eighth)
            turned[:, at] = weights[at, :].T
            return carry

        lax.fori_loop(first, last, step, 0)

    def arrive(ls, pieces):
        for s, dq in pieces:
            if dq and not (relay and dq == 3 - first_axis(s)):
                landed(s, peer(dq), ls)

    def project(ls, pieces, fresh):
        def step(j, carry):
            cols = pl.ds(pl.multiple_of(j * LANES, LANES), LANES)
            total = None if fresh else acc[:, cols]
            for s, dq in pieces:
                q = peer(dq)
                term = jnp.dot(
                    rows[s, q, ls],
                    weights[rows_of(s, q), cols],
                    preferred_element_type=jnp.float32,
                )
                total = term if total is None else total + term
            acc[:, cols] = total
            return carry

        lax.fori_loop(0, acc.shape[1] // LANES, step, 0)

    scaling = HD ** (-0.5)
    position = lax.broadcasted_iota(jnp.int32, (source, query_v.shape[1]), 0)

    def attend(ls):
        for s in range(sectors):
            view = got_len.at[ls, s]
            pltpu.make_async_copy(view, view, len_recv.at[ls, s]).wait()
        visible = position < got_len[ls, 0][0:1, :]
        for h in range(heads_w // HD):
            cols = slice(h * HD, (h + 1) * HD)
            wide = slice(heads_w + h * HD, heads_w + (h + 1) * HD)
            k = acc[:, cols].astype(jnp.bfloat16)
            v = acc[:, wide].astype(jnp.bfloat16)
            q = query_v[ls, :, cols]
            d = grad_v[ls, :, cols]
            scores = lax.dot_general(k, q, NT, preferred_element_type=jnp.float32) * scaling
            weights = jnp.where(visible, jnp.exp(scores), 0.0)
            probs = weights / jnp.sum(weights, axis=0, keepdims=True)
            grad_probs = lax.dot_general(v, d, NT, preferred_element_type=jnp.float32)
            deltas = jnp.sum(probs * grad_probs, axis=0, keepdims=True)
            grad_scores = (probs * (grad_probs - deltas) * scaling).astype(jnp.bfloat16)
            row_grads[:, cols] = jnp.dot(
                grad_scores, q, preferred_element_type=jnp.float32
            ).astype(jnp.bfloat16)
            row_grads[:, wide] = jnp.dot(
                probs.astype(jnp.bfloat16), d, preferred_element_type=jnp.float32
            ).astype(jnp.bfloat16)

    def part_copy(s, ls, dq):
        to = peer(dq)
        if relay:
            if isinstance(dq, int):
                to = peer(first_axis(s)) if dq == 3 else to
            else:
                to = jnp.where(dq == 3, peer(first_axis(s)), to)
        return pltpu.make_async_remote_copy(
            src_ref=part.at[dq - 1, s, ls],
            dst_ref=inbox.at[dq - 1, s, ls],
            send_sem=part_send.at[dq - 1, s, ls],
            recv_sem=part_recv.at[dq - 1, s, ls],
            device_id=(ms, ml, to),
            device_id_type=MESH,
        )

    def project_back(s, q):
        return jnp.dot(row_grads[...], turned[:, rows_of(s, q)], preferred_element_type=jnp.float32)

    held = 1 if relay else 0

    def backward(ls, way):
        def send(i, carry):
            step, s = lax.div(i, sectors), lax.rem(i, sectors)
            dq = quarters - 1 - step
            if relay:
                dq = jnp.where(step == 0, 3, first_axis(s))
            part[dq - 1, s, ls] = project_back(s, peer(dq)).astype(jnp.bfloat16)
            part_copy(s, ls, dq).start()
            return carry

        lax.fori_loop(0, sectors * (quarters - 1 - held), send, 0)

        def keep(i, carry):
            step, s = lax.div(i, sectors), lax.rem(i, sectors)
            dq = jnp.where(step == 0, 3 - first_axis(s), 0) if relay else 0
            own[held - step, s, way] = project_back(s, peer(dq))
            return carry

        lax.fori_loop(0, sectors * (1 + held), keep, 0)

    def part_landed(s, ls, dq):
        view = inbox.at[dq - 1, s, ls]
        pltpu.make_async_copy(view, view, part_recv.at[dq - 1, s, ls]).wait()
        return inbox[dq - 1, s, ls].astype(jnp.float32)

    def sum_on(ls, way):
        if relay:
            for s in range(sectors):
                dq = 3 - first_axis(s)
                total = own[1, s, way] + part_landed(s, ls, 3)
                part[dq - 1, s, ls] = total.astype(jnp.bfloat16)
                part_copy(s, ls, dq).start()

    def back_copy(s, ls):
        return pltpu.make_async_remote_copy(
            src_ref=reduced.at[s, ls],
            dst_ref=arrived.at[ml],
            send_sem=back_send.at[s, ls],
            recv_sem=back_recv.at[ml],
            device_id=(s, ms * half + ls, mq),
            device_id_type=MESH,
        )

    def local_back(s, ls):
        return pltpu.make_async_copy(reduced.at[s, ls], arrived.at[ml], back_recv.at[ml])

    def is_me(s, ls):
        return jnp.logical_and(s == ms, ms * half + ls == ml)

    def give_back(ls, way):
        for s in range(sectors):
            total = own[0, s, way]
            if relay:
                total = total + part_landed(s, ls, first_axis(s))
                total = total + part_landed(s, ls, 3 - first_axis(s))
            else:
                for dq in range(1, quarters):
                    total = total + part_landed(s, ls, dq)
            reduced[s, ls] = total.astype(jnp.bfloat16)

            @pl.when(is_me(s, ls))
            def _():
                local_back(s, ls).start()

            @pl.when(jnp.logical_not(is_me(s, ls)))
            def _():
                back_copy(s, ls).start()

    everything = [(s, dq) for dq in range(quarters) for s in range(sectors)]
    waves = [everything[: len(everything) // 2], everything[len(everything) // 2 :]]
    if relay:
        waves = [everything[: 2 * sectors], everything[2 * sectors : 3 * sectors], everything[3 * sectors :]]

    @pl.when(at_home)
    def _():
        for s in range(sectors):
            gather(slot_of(0), s)

    for load in loads:
        load.wait()
    turn(0, sectors * quarters // 2)

    @pl.when(jnp.logical_not(at_home))
    def _():
        for s in range(sectors):
            gather(slot_of(0), s)

    turn(sectors * quarters // 2, sectors * quarters)
    for s in range(sectors):
        pass_on(slot_of(0), s)
    for k in range(half):
        now, way = slot_of(k), k % 2
        if k + 1 < half:
            for s in range(sectors):
                gather(slot_of(k + 1), s)
        for n, wave in enumerate(waves):
            arrive(now, wave)
            project(now, wave, n == 0)
            if n == 0 and k > 0:
                sum_on(slot_of(k - 1), 1 - way)
        attend(now)
        if k + 1 < half:
            for s in range(sectors):
                pass_on(slot_of(k + 1), s)
        backward(now, way)
        if k > 0:
            give_back(slot_of(k - 1), 1 - way)
    sum_on(slot_of(half - 1), (half - 1) % 2)
    give_back(slot_of(half - 1), (half - 1) % 2)

    for g in range(groups):
        view = arrived.at[g]
        pltpu.make_async_copy(view, view, back_recv.at[g]).wait()
    for j in range(blocks):
        group = 0
        for c in range(languages):
            group = group + jnp.where(rank[c] == j, live[c] * group_of_lang[c], 0)
        out[0, j] = arrived[group]

    @pl.when(jnp.logical_not(at_home))
    def _():
        for copy in z_copy(0):
            copy.wait_send()

    for i in range(1, groups):
        for copy in z_copy(i):
            copy.wait_send()

    def drain(i, carry):
        ls, s = lax.rem(i, half), lax.div(i, half)
        for dq in range(1, quarters):
            mp_copy(s, ls, dq).wait_send()
            part_copy(s, ls, dq).wait_send()

        @pl.when(jnp.logical_not(is_me(s, ls)))
        def _():
            back_copy(s, ls).wait_send()

        return carry

    lax.fori_loop(0, sectors * half, drain, 0)


def body(memory, queries, out_grad, key_weight, value_weight, lang_rows, group_of_lang, src_len):
    blocks, source, eighth = memory.shape[1:]
    width, heads_w = key_weight.shape[1:]
    sectors, groups = lax.axis_size("sect"), lax.axis_size("lang")
    quarters = lax.axis_size("mp")
    half = groups // sectors
    dims = (sectors, groups, quarters, half, blocks, source, eighth, width, heads_w)
    low, full = jnp.bfloat16, jnp.float32
    vmem = pl.BlockSpec(memory_space=pltpu.VMEM)
    smem = pl.BlockSpec(memory_space=pltpu.SMEM)
    hbm = pl.BlockSpec(memory_space=pl.ANY)
    dma = pltpu.SemaphoreType.DMA
    scratch = [
        pltpu.VMEM((width, 2 * heads_w), low),
        pltpu.VMEM((2 * heads_w, width), low),
        pltpu.VMEM(memory.shape, low),
        pltpu.VMEM(queries.shape[1:], low),
        pltpu.VMEM(queries.shape[1:], low),
        pltpu.VMEM((groups, source, eighth), low),
        pltpu.VMEM((groups, 8, queries.shape[2]), jnp.int32),
        pltpu.VMEM((half, sectors, 8, queries.shape[2]), jnp.int32),
        pltpu.VMEM((sectors, quarters, half, source, eighth), low),
        pltpu.VMEM((source, 2 * heads_w), full),
        pltpu.VMEM((source, 2 * heads_w), low),
        pltpu.VMEM((quarters - 1, sectors, half, source, eighth), low),
        pltpu.VMEM((2, sectors, 2, source, eighth), full),
        pltpu.VMEM((quarters - 1, sectors, half, source, eighth), low),
        pltpu.VMEM((sectors, half, source, eighth), low),
        pltpu.VMEM((groups, source, eighth), low),
        dma((5,)),
        dma((groups,)),
        dma((groups,)),
        dma((half, sectors)),
        dma((sectors, quarters, half)),
        dma((quarters - 1, sectors, half)),
        dma((quarters - 1, sectors, half)),
        dma((quarters - 1, sectors, half)),
        dma((sectors, half)),
        dma((groups,)),
    ]
    return pl.pallas_call(
        functools.partial(kernel, dims),
        out_shape=jax.ShapeDtypeStruct(memory.shape, memory.dtype),
        in_specs=[smem, smem, smem, hbm, hbm, hbm, hbm, hbm],
        out_specs=vmem,
        scratch_shapes=scratch,
        compiler_params=pltpu.CompilerParams(
            collective_id=0, has_side_effects=True, vmem_limit_bytes=67043328
        ),
    )(lang_rows, group_of_lang, src_len, memory, queries, out_grad, key_weight, value_weight)


def solution(mesh):
    in_specs = (
        P("lang", None, None, ("sect", "mp")),
        P("lang", "sect", None, "mp"),
        P("lang", "sect", None, "mp"),
        P("lang", None, "mp"),
        P("lang", None, "mp"),
        P("lang", None),
        P(),
        P("lang", None),
    )
    out_specs = P("lang", None, None, ("sect", "mp"))
    return jax.shard_map(body, mesh=mesh, in_specs=in_specs, out_specs=out_specs, check_vma=False)
```

```python
import functools

import jax
import jax.numpy as jnp
from jax import lax
from jax.experimental import pallas as pl
from jax.experimental.pallas import tpu as pltpu
from jax.sharding import PartitionSpec as P

HD = 128
LANES = 256
MESH = pl.DeviceIdType.MESH
NT = (((1,), (1,)), ((), ()))


def kernel(
    dims,
    lang_rows,
    group_of_lang,
    src_len,
    memory_hbm,
    queries_hbm,
    grads_hbm,
    key_hbm,
    value_hbm,
    out,
    weights,
    turned,
    memory,
    query_v,
    grad_v,
    outgoing,
    out_len,
    got_len,
    rows,
    acc,
    acc_in,
    row_grads,
    part,
    own,
    inbox,
    reduced,
    arrived,
    load_sem,
    share_send,
    share_recv,
    z_send,
    z_len_send,
    len_recv,
    rows_recv,
    mp_send,
    acc_send,
    acc_recv,
    grads_send,
    grads_recv,
    part_send,
    part_recv,
    back_send,
    back_recv,
):
    sectors, groups, quarters, half, blocks, source, eighth, width, heads_w = dims
    ms, ml, mq = lax.axis_index("sect"), lax.axis_index("lang"), lax.axis_index("mp")
    languages = lang_rows.shape[1]
    mate = (1 - ms, ml, mq)
    mine_w = heads_w // sectors
    depth = width // sectors

    near = mq + 1 - 2 * lax.rem(mq, 2)
    far = mq + 2 - 4 * lax.div(mq, 2)
    first = jnp.where(ms == 0, near, far)
    second = jnp.where(ms == 0, far, near)
    across = quarters - 1 - mq

    side = jnp.where(ml < groups - 1 - ml, 1, -1)
    edge = jnp.minimum(ml, groups - 1 - ml)

    def nth(n):
        close = (n + 1) // 2 if n % 2 else -(n // 2)
        return ml + side * jnp.where(n <= 2 * edge, close, n - edge)

    fetch = pltpu.make_async_copy(memory_hbm, memory, load_sem.at[0])
    fetch.start()
    barrier = pltpu.get_barrier_semaphore()
    peers = [(ms, nth(n), mq) for n in range(groups - 1, 0, -1)]
    peers += [(ms, ml, near), (ms, ml, far), mate]
    for peer in peers:
        pl.semaphore_signal(barrier, inc=1, device_id=peer, device_id_type=MESH)

    loads = []
    rows_here = pl.ds(pl.multiple_of(ms * depth, depth), depth)
    for i, (ref, owner) in enumerate(
        [(key_hbm, ms), (value_hbm, ms), (key_hbm, 1 - ms), (value_hbm, 1 - ms)]
    ):
        cols = pl.ds(pl.multiple_of(owner * mine_w, mine_w), mine_w)
        loads.append(
            pltpu.make_async_copy(
                ref.at[0, rows_here, cols],
                weights.at[:, pl.ds(i * mine_w, mine_w)],
                load_sem.at[1 + i],
            )
        )
    cols_here = pl.ds(pl.multiple_of(ms * mine_w, mine_w), mine_w)
    cols_there = pl.ds(pl.multiple_of((1 - ms) * mine_w, mine_w), mine_w)
    shards_here = pl.ds(ms * half, half)
    shards_there = pl.ds((1 - ms) * half, half)
    pairs = [(queries_hbm, query_v), (grads_hbm, grad_v)]
    for i, (ref, held) in enumerate(pairs):
        loads.append(
            pltpu.make_async_copy(
                ref.at[0, :, :, cols_here], held.at[shards_here], load_sem.at[5 + i]
            )
        )
    for load in loads:
        load.start()

    live, rank, count = [], [], 0
    for c in range(languages):
        live.append((lang_rows[0, c] > 0).astype(jnp.int32))
        rank.append(count)
        count = count + live[c]
    fetch.wait()
    for n in range(groups):
        g = nth(n)
        index, routed = 0, 0
        for c in range(languages):
            hit = jnp.where(group_of_lang[c] == g, live[c], 0)
            index = index + hit * rank[c]
            routed = routed + hit
        length = jnp.maximum(jnp.where(routed > 0, src_len[0, index], 1), 1)
        if n == 0:
            rows[mq, ml] = memory[0, index]
            got_len[ml] = jnp.full(out_len.shape[1:], length, jnp.int32)
        else:
            outgoing[n] = memory[0, index]
            out_len[n] = jnp.full(out_len.shape[1:], length, jnp.int32)

    pl.semaphore_wait(barrier, groups - 1 + 3)

    def remote(src, dst, send, recv, to):
        return pltpu.make_async_remote_copy(
            src_ref=src,
            dst_ref=dst,
            send_sem=send,
            recv_sem=recv,
            device_id=to,
            device_id_type=MESH,
        )

    def landed(view, sem):
        pltpu.make_async_copy(view, view, sem).wait()

    def shift_copies(n):
        to = (ms, nth(n), mq)
        return (
            remote(outgoing.at[n], rows.at[mq, ml], z_send.at[n], rows_recv.at[mq, ml], to),
            remote(out_len.at[n], got_len.at[ml], z_len_send.at[n], len_recv.at[ml], to),
        )

    def shift(n):
        for copy in shift_copies(n):
            copy.start()

    def share_copies():
        return [
            remote(
                ref.at[0, :, :, cols_there],
                held.at[shards_here],
                share_send.at[i],
                share_recv.at[i],
                mate,
            )
            for i, (ref, held) in enumerate(pairs)
        ]

    def spread_copy(n, i):
        to = (ms, ml, (first, second, first)[i])
        q = second if i == 2 else mq
        view = rows.at[q, nth(n)]
        return remote(view, view, mp_send.at[i, n], rows_recv.at[q, nth(n)], to)

    def wait_rows(n, q):
        landed(rows.at[q, nth(n)], rows_recv.at[q, nth(n)])

    def gather(n):
        if n > 0:
            wait_rows(n, mq)
        spread_copy(n, 0).start()
        spread_copy(n, 1).start()

    def pass_on(n):
        wait_rows(n, second)
        spread_copy(n, 2).start()

    def rows_of(q):
        return pl.ds(pl.multiple_of(q * eighth, eighth), eighth)

    def turn(begin, end):
        def step(i, carry):
            turned[:, rows_of(i)] = weights[rows_of(i), :].T
            return carry

        lax.fori_loop(begin, end, step, 0)

    def acc_copy(n):
        return remote(acc.at[n % 2, 1], acc_in.at[n], acc_send.at[n], acc_recv.at[n], mate)

    def project(n, whose, sources, fresh):
        shard = nth(n)

        def step(j, carry):
            cols = pl.ds(pl.multiple_of(j * LANES, LANES), LANES)
            at = pl.ds(pl.multiple_of(whose * 2 * mine_w + j * LANES, LANES), LANES)
            total = None if fresh else acc[n % 2, whose, :, cols]
            for q in sources:
                term = jnp.dot(
                    rows[q, shard], weights[rows_of(q), at], preferred_element_type=jnp.float32
                )
                total = term if total is None else total + term
            acc[n % 2, whose, :, cols] = total
            return carry

        lax.fori_loop(0, 2 * mine_w // LANES, step, 0)

    def forward(n):
        if n >= 2:
            acc_copy(n - 2).wait_send()
        wait_rows(n, first)
        for whose in (1, 0):
            project(n, whose, (mq, second, first), True)
        wait_rows(n, across)
        project(n, 1, (across,), False)
        acc_copy(n).start()
        project(n, 0, (across,), False)

    scaling = HD ** (-0.5)
    position = lax.broadcasted_iota(jnp.int32, (source, query_v.shape[1]), 0)

    def grads_copy(n):
        return remote(
            row_grads.at[n, 0], row_grads.at[n, 1], grads_send.at[n], grads_recv.at[n], mate
        )

    def attend(n):
        shard = nth(n)
        if n > 0:
            landed(got_len.at[shard], len_recv.at[shard])
        landed(acc_in.at[n], acc_recv.at[n])
        visible = position < got_len[shard][0:1, :]
        for h in range(mine_w // HD):
            cols = slice(h * HD, (h + 1) * HD)
            wide = slice(mine_w + h * HD, mine_w + (h + 1) * HD)
            k = (acc[n % 2, 0, :, cols] + acc_in[n, :, cols]).astype(jnp.bfloat16)
            v = (acc[n % 2, 0, :, wide] + acc_in[n, :, wide]).astype(jnp.bfloat16)
            q = query_v[shard, :, cols]
            d = grad_v[shard, :, cols]
            scores = lax.dot_general(k, q, NT, preferred_element_type=jnp.float32) * scaling
            weight = jnp.where(visible, jnp.exp(scores), 0.0)
            probs = weight / jnp.sum(weight, axis=0, keepdims=True)
            grad_probs = lax.dot_general(v, d, NT, preferred_element_type=jnp.float32)
            deltas = jnp.sum(probs * grad_probs, axis=0, keepdims=True)
            grad_scores = (probs * (grad_probs - deltas) * scaling).astype(jnp.bfloat16)
            row_grads[n, 0, :, cols] = jnp.dot(
                grad_scores, q, preferred_element_type=jnp.float32
            ).astype(jnp.bfloat16)
            row_grads[n, 0, :, wide] = jnp.dot(
                probs.astype(jnp.bfloat16), d, preferred_element_type=jnp.float32
            ).astype(jnp.bfloat16)
        grads_copy(n).start()

    def part_copy(n, i):
        to = (ms, ml, second if i == 2 else first)
        return remote(
            part.at[i, n], inbox.at[i, n], part_send.at[i, n], part_recv.at[i, n], to
        )

    def part_landed(n, i):
        landed(inbox.at[i, n], part_recv.at[i, n])
        return inbox[i, n].astype(jnp.float32)

    def project_back(n, q):
        at = rows_of(q)
        return jnp.dot(
            row_grads[n, 0], turned[0 : 2 * mine_w, at], preferred_element_type=jnp.float32
        ) + jnp.dot(
            row_grads[n, 1], turned[2 * mine_w :, at], preferred_element_type=jnp.float32
        )

    def backward(n):
        way = n % 2
        landed(row_grads.at[n, 1], grads_recv.at[n])
        for i, q in enumerate((across, first)):
            part[i, n] = project_back(n, q).astype(jnp.bfloat16)
            part_copy(n, i).start()
        own[1, way] = project_back(n, second)
        own[0, way] = project_back(n, mq)

    def sum_on(n):
        part[2, n] = (own[1, n % 2] + part_landed(n, 0)).astype(jnp.bfloat16)
        part_copy(n, 2).start()

    def back_copy(n):
        return remote(
            reduced.at[n], arrived.at[ml], back_send.at[n], back_recv.at[ml], (ms, nth(n), mq)
        )

    def give_back(n):
        total = own[0, n % 2] + part_landed(n, 1)
        total = (total + part_landed(n, 2)).astype(jnp.bfloat16)
        if n == 0:
            arrived[ml] = total
        else:
            reduced[n] = total
            back_copy(n).start()

    shift(1)
    gather(0)
    inner = edge > 0

    @pl.when(inner)
    def _():
        for n in range(2, groups):
            shift(n)

    for copy in share_copies():
        copy.start()
    for load in loads:
        load.wait()
    turn(0, quarters // 2)
    pass_on(0)
    gather(1)

    @pl.when(jnp.logical_not(inner))
    def _():
        for n in range(2, groups):
            shift(n)

    turn(quarters // 2, quarters)
    for i, (_, held) in enumerate(pairs):
        landed(held.at[shards_there], share_recv.at[i])
    for n in range(groups):
        forward(n)
        if n + 1 < groups:
            pass_on(n + 1)
        if n + 2 < groups:
            gather(n + 2)
        if n >= 2:
            sum_on(n - 1)
        attend(n)
        if n >= 1:
            backward(n)
        if n >= 2:
            give_back(n - 1)
    backward(0)
    sum_on(groups - 1)
    give_back(groups - 1)
    sum_on(0)
    give_back(0)

    for n in range(1, groups):
        g = nth(n)
        landed(arrived.at[g], back_recv.at[g])
    for j in range(blocks):
        group = 0
        for c in range(languages):
            group = group + jnp.where(rank[c] == j, live[c] * group_of_lang[c], 0)
        out[0, j] = arrived[group]

    for copy in share_copies():
        copy.wait_send()
    for n in range(groups):
        if n > 0:
            for copy in shift_copies(n):
                copy.wait_send()
            back_copy(n).wait_send()
        for i in range(3):
            spread_copy(n, i).wait_send()
            part_copy(n, i).wait_send()
        if n >= groups - 2:
            acc_copy(n).wait_send()
        grads_copy(n).wait_send()


def body(memory, queries, out_grad, key_weight, value_weight, lang_rows, group_of_lang, src_len):
    blocks, source, eighth = memory.shape[1:]
    width, heads_w = key_weight.shape[1:]
    sectors, groups = lax.axis_size("sect"), lax.axis_size("lang")
    quarters = lax.axis_size("mp")
    half, target = queries.shape[1:3]
    mine_w, depth = heads_w // sectors, width // sectors
    assert sectors == 2 and quarters == 4 and groups >= 2
    dims = (sectors, groups, quarters, half, blocks, source, eighth, width, heads_w)
    low, full = jnp.bfloat16, jnp.float32
    vmem = pl.BlockSpec(memory_space=pltpu.VMEM)
    smem = pl.BlockSpec(memory_space=pltpu.SMEM)
    hbm = pl.BlockSpec(memory_space=pl.ANY)
    dma = pltpu.SemaphoreType.DMA
    scratch = [
        pltpu.VMEM((depth, 2 * heads_w), low),
        pltpu.VMEM((2 * heads_w, depth), low),
        pltpu.VMEM(memory.shape, low),
        pltpu.VMEM((groups, target, mine_w), low),
        pltpu.VMEM((groups, target, mine_w), low),
        pltpu.VMEM((groups, source, eighth), low),
        pltpu.VMEM((groups, 8, target), jnp.int32),
        pltpu.VMEM((groups, 8, target), jnp.int32),
        pltpu.VMEM((quarters, groups, source, eighth), low),
        pltpu.VMEM((2, 2, source, 2 * mine_w), full),
        pltpu.VMEM((groups, source, 2 * mine_w), full),
        pltpu.VMEM((groups, 2, source, 2 * mine_w), low),
        pltpu.VMEM((3, groups, source, eighth), low),
        pltpu.VMEM((2, 2, source, eighth), full),
        pltpu.VMEM((3, groups, source, eighth), low),
        pltpu.VMEM((groups, source, eighth), low),
        pltpu.VMEM((groups, source, eighth), low),
        dma((7,)),
        dma((2,)),
        dma((2,)),
        dma((groups,)),
        dma((groups,)),
        dma((groups,)),
        dma((quarters, groups)),
        dma((3, groups)),
        dma((groups,)),
        dma((groups,)),
        dma((groups,)),
        dma((groups,)),
        dma((3, groups)),
        dma((3, groups)),
        dma((groups,)),
        dma((groups,)),
    ]
    return pl.pallas_call(
        functools.partial(kernel, dims),
        out_shape=jax.ShapeDtypeStruct(memory.shape, memory.dtype),
        in_specs=[smem, smem, smem, hbm, hbm, hbm, hbm, hbm],
        out_specs=vmem,
        scratch_shapes=scratch,
        compiler_params=pltpu.CompilerParams(
            collective_id=0, has_side_effects=True, vmem_limit_bytes=67043328
        ),
    )(lang_rows, group_of_lang, src_len, memory, queries, out_grad, key_weight, value_weight)


def solution(mesh):
    in_specs = (
        P("lang", None, None, ("sect", "mp")),
        P("lang", "sect", None, "mp"),
        P("lang", "sect", None, "mp"),
        P("lang", None, "mp"),
        P("lang", None, "mp"),
        P("lang", None),
        P(),
        P("lang", None),
    )
    out_specs = P("lang", None, None, ("sect", "mp"))
    return jax.shard_map(body, mesh=mesh, in_specs=in_specs, out_specs=out_specs, check_vma=False)
```

```python
import functools

import jax
import jax.numpy as jnp
from jax import lax
from jax.experimental import pallas as pl
from jax.experimental.pallas import tpu as pltpu
from jax.sharding import PartitionSpec as P

HD = 128
LANES = 256
CHUNKS = 2
PLAN = (
    ("shift_near", 0),
    ("gather", 0, 0),
    ("gather", 0, 1),
    ("shift_inner", 0),
    ("share", 0),
    ("turn", 0),
    ("turn", 1),
    ("pass_on", 0, 0),
    ("pass_on", 0, 1),
    ("gather", 1, 0),
    ("gather", 1, 1),
    ("shift_outer", 0),
    ("turn", 2),
    ("turn", 3),
    ("project", 0),
    ("finish", 0),
    ("pass_on", 1, 0),
    ("gather", 2, 0),
    ("pass_on", 1, 1),
    ("gather", 2, 1),
    ("attend", 0),
    ("project", 1),
    ("finish", 1),
    ("pass_on", 2, 0),
    ("gather", 3, 0),
    ("pass_on", 2, 1),
    ("gather", 3, 1),
    ("attend", 1),
    ("send_back", 1),
    ("keep_back", 1),
    ("project", 2),
    ("finish", 2),
    ("pass_on", 3, 0),
    ("pass_on", 3, 1),
    ("sum_on", 1, 0),
    ("sum_on", 1, 1),
    ("attend", 2),
    ("send_back", 2),
    ("keep_back", 2),
    ("give_back", 1, 0),
    ("give_back", 1, 1),
    ("project", 3),
    ("finish", 3),
    ("sum_on", 2, 0),
    ("sum_on", 2, 1),
    ("attend", 3),
    ("send_back", 3),
    ("keep_back", 3),
    ("give_back", 2, 0),
    ("give_back", 2, 1),
    ("send_back", 0),
    ("keep_back", 0),
    ("sum_on", 3, 0),
    ("sum_on", 3, 1),
    ("give_back", 3, 0),
    ("give_back", 3, 1),
    ("sum_on", 0, 0),
    ("sum_on", 0, 1),
    ("give_back", 0, 0),
    ("give_back", 0, 1),
)
EXTRA = (
    "gather",
    "pass_on",
    "project",
    "finish",
    "attend",
    "send_back",
    "keep_back",
    "sum_on",
    "give_back",
)
PARTED = ("gather", "pass_on", "sum_on", "give_back")
LEAD = ("shift_near", "shift_inner", "shift_outer", "share", "turn")
MESH = pl.DeviceIdType.MESH
NT = (((1,), (1,)), ((), ()))


def kernel(
    dims,
    lang_rows,
    group_of_lang,
    src_len,
    memory_hbm,
    queries_hbm,
    grads_hbm,
    key_hbm,
    value_hbm,
    out,
    weights,
    turned,
    memory,
    query_v,
    grad_v,
    outgoing,
    out_len,
    got_len,
    rows,
    acc,
    acc_in,
    row_grads,
    part,
    own,
    inbox,
    reduced,
    arrived,
    load_sem,
    share_send,
    share_recv,
    z_send,
    z_len_send,
    len_recv,
    rows_recv,
    mp_send,
    acc_send,
    acc_recv,
    grads_send,
    grads_recv,
    part_send,
    part_recv,
    back_send,
    back_recv,
):
    sectors, groups, quarters, half, blocks, source, eighth, width, heads_w = dims
    ms, ml, mq = lax.axis_index("sect"), lax.axis_index("lang"), lax.axis_index("mp")
    languages = lang_rows.shape[1]
    mate = (1 - ms, ml, mq)
    mine_w = heads_w // sectors
    depth = width // sectors

    near = mq + 1 - 2 * lax.rem(mq, 2)
    far = mq + 2 - 4 * lax.div(mq, 2)
    first = jnp.where(ms == 0, near, far)
    second = jnp.where(ms == 0, far, near)
    across = quarters - 1 - mq

    side = jnp.where(ml < groups - 1 - ml, 1, -1)
    edge = jnp.minimum(ml, groups - 1 - ml)

    def sent(n):
        close = (n + 1) // 2 if n % 2 else -(n // 2)
        return ml + side * jnp.where(n <= 2 * edge, close, n - edge)

    far_end = jnp.maximum(2 * edge, 1) + 1

    def nth(n):
        close = (n + 1) // 2 if n % 2 else -(n // 2)
        beyond = far_end + groups - 1 - n - edge
        return ml + side * jnp.where(n < far_end, jnp.where(n <= 2 * edge, close, n - edge), beyond)

    fetch = pltpu.make_async_copy(memory_hbm, memory, load_sem.at[0])
    fetch.start()
    barrier = pltpu.get_barrier_semaphore()
    peers = [(ms, nth(n), mq) for n in range(groups - 1, 0, -1)]
    peers += [(ms, ml, near), (ms, ml, far), mate]
    for peer in peers:
        pl.semaphore_signal(barrier, inc=1, device_id=peer, device_id_type=MESH)

    loads = []
    rows_here = pl.ds(pl.multiple_of(ms * depth, depth), depth)
    for i, (ref, owner) in enumerate(
        [(key_hbm, ms), (value_hbm, ms), (key_hbm, 1 - ms), (value_hbm, 1 - ms)]
    ):
        cols = pl.ds(pl.multiple_of(owner * mine_w, mine_w), mine_w)
        loads.append(
            pltpu.make_async_copy(
                ref.at[0, rows_here, cols],
                weights.at[:, pl.ds(i * mine_w, mine_w)],
                load_sem.at[1 + i],
            )
        )
    cols_here = pl.ds(pl.multiple_of(ms * mine_w, mine_w), mine_w)
    cols_there = pl.ds(pl.multiple_of((1 - ms) * mine_w, mine_w), mine_w)
    shards_here = pl.ds(ms * half, half)
    shards_there = pl.ds((1 - ms) * half, half)
    pairs = [(queries_hbm, query_v), (grads_hbm, grad_v)]
    for i, (ref, held) in enumerate(pairs):
        loads.append(
            pltpu.make_async_copy(
                ref.at[0, :, :, cols_here], held.at[shards_here], load_sem.at[5 + i]
            )
        )
    for load in loads:
        load.start()

    live, rank, count = [], [], 0
    for c in range(languages):
        live.append((lang_rows[0, c] > 0).astype(jnp.int32))
        rank.append(count)
        count = count + live[c]
    fetch.wait()
    for n in range(groups):
        g = sent(n)
        index, routed = 0, 0
        for c in range(languages):
            hit = jnp.where(group_of_lang[c] == g, live[c], 0)
            index = index + hit * rank[c]
            routed = routed + hit
        length = jnp.maximum(jnp.where(routed > 0, src_len[0, index], 1), 1)
        if n == 0:
            rows[mq, ml] = memory[0, index]
            got_len[ml] = jnp.full(out_len.shape[1:], length, jnp.int32)
        else:
            outgoing[n] = memory[0, index]
            out_len[n] = jnp.full(out_len.shape[1:], length, jnp.int32)

    pl.semaphore_wait(barrier, groups - 1 + 3)

    def way(n):
        return 0 if n == 0 else 1 + (n - 1) % 3

    def remote(src, dst, send, recv, to):
        return pltpu.make_async_remote_copy(
            src_ref=src,
            dst_ref=dst,
            send_sem=send,
            recv_sem=recv,
            device_id=to,
            device_id_type=MESH,
        )

    def landed(view, sem):
        pltpu.make_async_copy(view, view, sem).wait()

    size = source // CHUNKS
    chunks = range(CHUNKS)

    def lines(c):
        return pl.ds(c * size, size)

    def shift_copies(n):
        to = (ms, sent(n), mq)
        return [
            remote(
                outgoing.at[n, lines(c)],
                rows.at[mq, ml, lines(c)],
                z_send.at[n, c],
                rows_recv.at[mq, ml, c],
                to,
            )
            for c in chunks
        ] + [remote(out_len.at[n], got_len.at[ml], z_len_send.at[n], len_recv.at[ml], to)]

    def shift(n):
        for copy in shift_copies(n):
            copy.start()

    def share_copies():
        return [
            remote(
                ref.at[0, :, :, cols_there],
                held.at[shards_here],
                share_send.at[i],
                share_recv.at[i],
                mate,
            )
            for i, (ref, held) in enumerate(pairs)
        ]

    def spread_copy(n, i, c):
        to = (ms, ml, (first, second, first)[i])
        q = second if i == 2 else mq
        view = rows.at[q, nth(n), lines(c)]
        return remote(view, view, mp_send.at[i, n, c], rows_recv.at[q, nth(n), c], to)

    def wait_rows(n, q, c):
        landed(rows.at[q, nth(n), lines(c)], rows_recv.at[q, nth(n), c])

    def gather(n, c):
        if n > 0:
            wait_rows(n, mq, c)
        spread_copy(n, 0, c).start()
        spread_copy(n, 1, c).start()

    def pass_on(n, c):
        wait_rows(n, second, c)
        spread_copy(n, 2, c).start()

    def rows_of(q):
        return pl.ds(pl.multiple_of(q * eighth, eighth), eighth)

    def turn(begin, end):
        def step(i, carry):
            turned[:, rows_of(i)] = weights[rows_of(i), :].T
            return carry

        lax.fori_loop(begin, end, step, 0)

    def acc_copy(n):
        return remote(acc.at[way(n), 1], acc_in.at[n], acc_send.at[n], acc_recv.at[n], mate)

    def multiply(n, whose, sources, fresh):
        shard = nth(n)

        def step(j, carry):
            cols = pl.ds(pl.multiple_of(j * LANES, LANES), LANES)
            at = pl.ds(pl.multiple_of(whose * 2 * mine_w + j * LANES, LANES), LANES)
            total = None if fresh else acc[way(n), whose, :, cols]
            for q in sources:
                term = jnp.dot(
                    rows[q, shard], weights[rows_of(q), at], preferred_element_type=jnp.float32
                )
                total = term if total is None else total + term
            acc[way(n), whose, :, cols] = total
            return carry

        lax.fori_loop(0, 2 * mine_w // LANES, step, 0)

    def project(n):
        if n > 3:
            acc_copy(n - 3).wait_send()
        for c in chunks:
            wait_rows(n, first, c)
        for whose in (1, 0):
            multiply(n, whose, (mq, second, first), True)

    def finish(n):
        for c in chunks:
            wait_rows(n, across, c)
        multiply(n, 1, (across,), False)
        acc_copy(n).start()
        multiply(n, 0, (across,), False)

    scaling = HD ** (-0.5)
    position = lax.broadcasted_iota(jnp.int32, (source, query_v.shape[1]), 0)

    def grads_copy(n):
        return remote(
            row_grads.at[n, 0], row_grads.at[n, 1], grads_send.at[n], grads_recv.at[n], mate
        )

    def attend(n):
        shard = nth(n)
        if n > 0:
            landed(got_len.at[shard], len_recv.at[shard])
        landed(acc_in.at[n], acc_recv.at[n])
        visible = position < got_len[shard][0:1, :]
        for h in range(mine_w // HD):
            cols = slice(h * HD, (h + 1) * HD)
            wide = slice(mine_w + h * HD, mine_w + (h + 1) * HD)
            k = (acc[way(n), 0, :, cols] + acc_in[n, :, cols]).astype(jnp.bfloat16)
            v = (acc[way(n), 0, :, wide] + acc_in[n, :, wide]).astype(jnp.bfloat16)
            q = query_v[shard, :, cols]
            d = grad_v[shard, :, cols]
            scores = lax.dot_general(k, q, NT, preferred_element_type=jnp.float32) * scaling
            weight = jnp.where(visible, jnp.exp(scores), 0.0)
            probs = weight / jnp.sum(weight, axis=0, keepdims=True)
            grad_probs = lax.dot_general(v, d, NT, preferred_element_type=jnp.float32)
            deltas = jnp.sum(probs * grad_probs, axis=0, keepdims=True)
            grad_scores = (probs * (grad_probs - deltas) * scaling).astype(jnp.bfloat16)
            row_grads[n, 0, :, cols] = jnp.dot(
                grad_scores, q, preferred_element_type=jnp.float32
            ).astype(jnp.bfloat16)
            row_grads[n, 0, :, wide] = jnp.dot(
                probs.astype(jnp.bfloat16), d, preferred_element_type=jnp.float32
            ).astype(jnp.bfloat16)
        grads_copy(n).start()

    def part_copy(n, i, c):
        to = (ms, ml, second if i == 2 else first)
        return remote(
            part.at[i, n, lines(c)],
            inbox.at[i, n, lines(c)],
            part_send.at[i, n, c],
            part_recv.at[i, n, c],
            to,
        )

    def part_landed(n, i, c):
        landed(inbox.at[i, n, lines(c)], part_recv.at[i, n, c])
        return inbox[i, n, lines(c)].astype(jnp.float32)

    def project_back(n, q):
        at = rows_of(q)
        return jnp.dot(
            row_grads[n, 0], turned[0 : 2 * mine_w, at], preferred_element_type=jnp.float32
        ) + jnp.dot(
            row_grads[n, 1], turned[2 * mine_w :, at], preferred_element_type=jnp.float32
        )

    def send_back(n):
        landed(row_grads.at[n, 1], grads_recv.at[n])
        for i, q in enumerate((across, first)):
            part[i, n] = project_back(n, q).astype(jnp.bfloat16)
            for c in chunks:
                part_copy(n, i, c).start()

    def keep_back(n):
        own[1, way(n)] = project_back(n, second)
        own[0, way(n)] = project_back(n, mq)

    def sum_on(n, c):
        kept = own[1, way(n), lines(c)]
        part[2, n, lines(c)] = (kept + part_landed(n, 0, c)).astype(jnp.bfloat16)
        part_copy(n, 2, c).start()

    def back_copy(n, c):
        return remote(
            reduced.at[n, lines(c)],
            arrived.at[ml, lines(c)],
            back_send.at[n, c],
            back_recv.at[ml, c],
            (ms, nth(n), mq),
        )

    def give_back(n, c):
        total = own[0, way(n), lines(c)] + part_landed(n, 1, c)
        total = (total + part_landed(n, 2, c)).astype(jnp.bfloat16)
        if n == 0:
            arrived[ml, lines(c)] = total
        else:
            reduced[n, lines(c)] = total
            back_copy(n, c).start()

    inner = edge > 0

    def shift_rest(when):
        @pl.when(when)
        def _():
            for n in range(2, groups):
                shift(n)

    def share():
        for copy in share_copies():
            copy.start()

    rest = list(loads)

    def loaded():
        while rest:
            rest.pop(0).wait()

    def project_loaded(n):
        loaded()
        project(n)

    def turn_loaded(i):
        loaded()
        turn(i, i + 1)

    shared = list(enumerate(pairs))

    def attend_shared(n):
        while shared:
            i, (_, held) = shared.pop(0)
            landed(held.at[shards_there], share_recv.at[i])
        attend(n)

    steps = {
        "shift_near": lambda n: shift(1),
        "shift_inner": lambda n: shift_rest(inner),
        "shift_outer": lambda n: shift_rest(jnp.logical_not(inner)),
        "share": lambda n: share(),
        "turn": turn_loaded,
        "gather": gather,
        "pass_on": pass_on,
        "project": project_loaded,
        "finish": finish,
        "attend": attend_shared,
        "send_back": send_back,
        "keep_back": keep_back,
        "sum_on": sum_on,
        "give_back": give_back,
    }
    skip = groups - 4
    plan = [
        (name, n if name == "turn" or n == 0 else n + skip, *c) for name, n, *c in PLAN
    ]
    if skip > 0:
        lead = [step for step in plan if step[0] in LEAD]
        rest_of = [step for step in plan if step[0] not in LEAD]
        extra = []
        for n in range(1, skip + 1):
            for name in EXTRA:
                extra += [(name, n, c) for c in chunks] if name in PARTED else [(name, n)]
        plan = lead + extra + rest_of
    for name, n, *c in plan:
        steps[name](n, *c)

    for n in range(1, groups):
        g = nth(n)
        for c in chunks:
            landed(arrived.at[g, lines(c)], back_recv.at[g, c])
    for j in range(blocks):
        group = 0
        for c in range(languages):
            group = group + jnp.where(rank[c] == j, live[c] * group_of_lang[c], 0)
        out[0, j] = arrived[group]

    for copy in share_copies():
        copy.wait_send()
    for n in range(groups):
        if n > 0:
            for copy in shift_copies(n):
                copy.wait_send()
            for c in chunks:
                back_copy(n, c).wait_send()
        for i in range(3):
            for c in chunks:
                spread_copy(n, i, c).wait_send()
                part_copy(n, i, c).wait_send()
        if n == 0 or n > groups - 4:
            acc_copy(n).wait_send()
        grads_copy(n).wait_send()


def body(memory, queries, out_grad, key_weight, value_weight, lang_rows, group_of_lang, src_len):
    blocks, source, eighth = memory.shape[1:]
    width, heads_w = key_weight.shape[1:]
    sectors, groups = lax.axis_size("sect"), lax.axis_size("lang")
    quarters = lax.axis_size("mp")
    half, target = queries.shape[1:3]
    mine_w, depth = heads_w // sectors, width // sectors
    assert sectors == 2 and quarters == 4 and groups >= 2
    dims = (sectors, groups, quarters, half, blocks, source, eighth, width, heads_w)
    low, full = jnp.bfloat16, jnp.float32
    vmem = pl.BlockSpec(memory_space=pltpu.VMEM)
    smem = pl.BlockSpec(memory_space=pltpu.SMEM)
    hbm = pl.BlockSpec(memory_space=pl.ANY)
    dma = pltpu.SemaphoreType.DMA
    scratch = [
        pltpu.VMEM((depth, 2 * heads_w), low),
        pltpu.VMEM((2 * heads_w, depth), low),
        pltpu.VMEM(memory.shape, low),
        pltpu.VMEM((groups, target, mine_w), low),
        pltpu.VMEM((groups, target, mine_w), low),
        pltpu.VMEM((groups, source, eighth), low),
        pltpu.VMEM((groups, 8, target), jnp.int32),
        pltpu.VMEM((groups, 8, target), jnp.int32),
        pltpu.VMEM((quarters, groups, source, eighth), low),
        pltpu.VMEM((4, 2, source, 2 * mine_w), full),
        pltpu.VMEM((groups, source, 2 * mine_w), full),
        pltpu.VMEM((groups, 2, source, 2 * mine_w), low),
        pltpu.VMEM((3, groups, source, eighth), low),
        pltpu.VMEM((2, 4, source, eighth), full),
        pltpu.VMEM((3, groups, source, eighth), low),
        pltpu.VMEM((groups, source, eighth), low),
        pltpu.VMEM((groups, source, eighth), low),
        dma((7,)),
        dma((2,)),
        dma((2,)),
        dma((groups, CHUNKS)),
        dma((groups,)),
        dma((groups,)),
        dma((quarters, groups, CHUNKS)),
        dma((3, groups, CHUNKS)),
        dma((groups,)),
        dma((groups,)),
        dma((groups,)),
        dma((groups,)),
        dma((3, groups, CHUNKS)),
        dma((3, groups, CHUNKS)),
        dma((groups, CHUNKS)),
        dma((groups, CHUNKS)),
    ]
    return pl.pallas_call(
        functools.partial(kernel, dims),
        out_shape=jax.ShapeDtypeStruct(memory.shape, memory.dtype),
        in_specs=[smem, smem, smem, hbm, hbm, hbm, hbm, hbm],
        out_specs=vmem,
        scratch_shapes=scratch,
        compiler_params=pltpu.CompilerParams(
            collective_id=0, has_side_effects=True, vmem_limit_bytes=67043328
        ),
    )(lang_rows, group_of_lang, src_len, memory, queries, out_grad, key_weight, value_weight)


def solution(mesh):
    in_specs = (
        P("lang", None, None, ("sect", "mp")),
        P("lang", "sect", None, "mp"),
        P("lang", "sect", None, "mp"),
        P("lang", None, "mp"),
        P("lang", None, "mp"),
        P("lang", None),
        P(),
        P("lang", None),
    )
    out_specs = P("lang", None, None, ("sect", "mp"))
    return jax.shard_map(body, mesh=mesh, in_specs=in_specs, out_specs=out_specs, check_vma=False)
```

```python
import functools

import jax
import jax.numpy as jnp
from jax import lax
from jax.experimental import pallas as pl
from jax.experimental.pallas import tpu as pltpu
from jax.sharding import PartitionSpec as P

HD = 128
LANES = 256
CHUNKS = 2
PLAN = (
    ("shift_near", 0),
    ("gather", 0, 0),
    ("gather", 0, 1),
    ("shift_inner", 0),
    ("share", 0),
    ("turn", 0),
    ("turn", 1),
    ("pass_on", 0, 0),
    ("pass_on", 0, 1),
    ("gather", 1, 0),
    ("gather", 1, 1),
    ("shift_outer", 0),
    ("turn", 2),
    ("turn", 3),
    ("project", 0),
    ("finish", 0),
    ("pass_on", 1, 0),
    ("gather", 2, 0),
    ("pass_on", 1, 1),
    ("gather", 2, 1),
    ("attend", 0),
    ("project", 1),
    ("finish", 1),
    ("pass_on", 2, 0),
    ("gather", 3, 0),
    ("pass_on", 2, 1),
    ("gather", 3, 1),
    ("attend", 1),
    ("send_back", 1),
    ("keep_back", 1),
    ("project", 2),
    ("finish", 2),
    ("pass_on", 3, 0),
    ("pass_on", 3, 1),
    ("sum_on", 1, 0),
    ("sum_on", 1, 1),
    ("attend", 2),
    ("send_back", 2),
    ("keep_back", 2),
    ("give_back", 1, 0),
    ("give_back", 1, 1),
    ("project", 3),
    ("finish", 3),
    ("sum_on", 2, 0),
    ("sum_on", 2, 1),
    ("attend", 3),
    ("send_back", 3),
    ("keep_back", 3),
    ("give_back", 2, 0),
    ("give_back", 2, 1),
    ("send_back", 0),
    ("keep_back", 0),
    ("sum_on", 3, 0),
    ("sum_on", 3, 1),
    ("give_back", 3, 0),
    ("give_back", 3, 1),
    ("sum_on", 0, 0),
    ("sum_on", 0, 1),
    ("give_back", 0, 0),
    ("give_back", 0, 1),
)
EXTRA = (
    "gather",
    "pass_on",
    "project",
    "finish",
    "attend",
    "send_back",
    "keep_back",
    "sum_on",
    "give_back",
)
PARTED = ("gather", "pass_on", "sum_on", "give_back")
LEAD = ("shift_near", "shift_inner", "shift_outer", "share", "turn")
MESH = pl.DeviceIdType.MESH
NT = (((1,), (1,)), ((), ()))


def kernel(
    dims,
    lang_rows,
    group_of_lang,
    src_len,
    memory_hbm,
    queries_hbm,
    grads_hbm,
    key_hbm,
    value_hbm,
    out,
    weights,
    turned,
    memory,
    query_v,
    grad_v,
    outgoing,
    out_len,
    got_len,
    rows,
    acc,
    acc_out,
    acc_in,
    row_grads,
    part,
    own,
    inbox,
    reduced,
    arrived,
    load_sem,
    share_send,
    share_recv,
    z_send,
    z_len_send,
    len_recv,
    rows_recv,
    mp_send,
    acc_send,
    acc_recv,
    grads_send,
    grads_recv,
    part_send,
    part_recv,
    back_send,
    back_recv,
):
    sectors, groups, quarters, half, blocks, source, eighth, width, heads_w = dims
    ms, ml, mq = lax.axis_index("sect"), lax.axis_index("lang"), lax.axis_index("mp")
    languages = lang_rows.shape[1]
    mate = (1 - ms, ml, mq)
    mine_w = heads_w // sectors
    depth = width // sectors

    near = mq + 1 - 2 * lax.rem(mq, 2)
    far = mq + 2 - 4 * lax.div(mq, 2)
    first = jnp.where(ms == 0, near, far)
    second = jnp.where(ms == 0, far, near)
    across = quarters - 1 - mq

    side = jnp.where(ml < groups - 1 - ml, 1, -1)
    edge = jnp.minimum(ml, groups - 1 - ml)

    def sent(n):
        close = (n + 1) // 2 if n % 2 else -(n // 2)
        return ml + side * jnp.where(n <= 2 * edge, close, n - edge)

    far_end = jnp.maximum(2 * edge, 1) + 1

    def nth(n):
        close = (n + 1) // 2 if n % 2 else -(n // 2)
        beyond = far_end + groups - 1 - n - edge
        return ml + side * jnp.where(n < far_end, jnp.where(n <= 2 * edge, close, n - edge), beyond)

    fetch = pltpu.make_async_copy(memory_hbm, memory, load_sem.at[0])
    fetch.start()
    barrier = pltpu.get_barrier_semaphore()
    peers = [(ms, nth(n), mq) for n in range(groups - 1, 0, -1)]
    peers += [(ms, ml, near), (ms, ml, far), mate]
    for peer in peers:
        pl.semaphore_signal(barrier, inc=1, device_id=peer, device_id_type=MESH)

    loads = []
    rows_here = pl.ds(pl.multiple_of(ms * depth, depth), depth)
    for i, (ref, owner) in enumerate(
        [(key_hbm, ms), (value_hbm, ms), (key_hbm, 1 - ms), (value_hbm, 1 - ms)]
    ):
        cols = pl.ds(pl.multiple_of(owner * mine_w, mine_w), mine_w)
        loads.append(
            pltpu.make_async_copy(
                ref.at[0, rows_here, cols],
                weights.at[:, pl.ds(i * mine_w, mine_w)],
                load_sem.at[1 + i],
            )
        )
    cols_here = pl.ds(pl.multiple_of(ms * mine_w, mine_w), mine_w)
    cols_there = pl.ds(pl.multiple_of((1 - ms) * mine_w, mine_w), mine_w)
    shards_here = pl.ds(ms * half, half)
    shards_there = pl.ds((1 - ms) * half, half)
    pairs = [(queries_hbm, query_v), (grads_hbm, grad_v)]
    for i, (ref, held) in enumerate(pairs):
        loads.append(
            pltpu.make_async_copy(
                ref.at[0, :, :, cols_here], held.at[shards_here], load_sem.at[5 + i]
            )
        )
    for load in loads:
        load.start()

    live, rank, count = [], [], 0
    for c in range(languages):
        live.append((lang_rows[0, c] > 0).astype(jnp.int32))
        rank.append(count)
        count = count + live[c]
    fetch.wait()
    for n in range(groups):
        g = sent(n)
        index, routed = 0, 0
        for c in range(languages):
            hit = jnp.where(group_of_lang[c] == g, live[c], 0)
            index = index + hit * rank[c]
            routed = routed + hit
        length = jnp.maximum(jnp.where(routed > 0, src_len[0, index], 1), 1)
        if n == 0:
            rows[mq, ml] = memory[0, index]
            got_len[ml] = jnp.full(out_len.shape[1:], length, jnp.int32)
        else:
            outgoing[n] = memory[0, index]
            out_len[n] = jnp.full(out_len.shape[1:], length, jnp.int32)

    pl.semaphore_wait(barrier, groups - 1 + 3)

    def way(n):
        return 0 if n == 0 else 1 + (n - 1) % 3

    def remote(src, dst, send, recv, to):
        return pltpu.make_async_remote_copy(
            src_ref=src,
            dst_ref=dst,
            send_sem=send,
            recv_sem=recv,
            device_id=to,
            device_id_type=MESH,
        )

    def landed(view, sem):
        pltpu.make_async_copy(view, view, sem).wait()

    size = source // CHUNKS
    chunks = range(CHUNKS)

    def lines(c):
        return pl.ds(c * size, size)

    def shift_copies(n):
        to = (ms, sent(n), mq)
        return [
            remote(
                outgoing.at[n, lines(c)],
                rows.at[mq, ml, lines(c)],
                z_send.at[n, c],
                rows_recv.at[mq, ml, c],
                to,
            )
            for c in chunks
        ] + [remote(out_len.at[n], got_len.at[ml], z_len_send.at[n], len_recv.at[ml], to)]

    def shift(n):
        for copy in shift_copies(n):
            copy.start()

    def share_copies():
        return [
            remote(
                ref.at[0, :, :, cols_there],
                held.at[shards_here],
                share_send.at[i],
                share_recv.at[i],
                mate,
            )
            for i, (ref, held) in enumerate(pairs)
        ]

    def spread_copy(n, i, c):
        to = (ms, ml, (first, second, first)[i])
        q = second if i == 2 else mq
        view = rows.at[q, nth(n), lines(c)]
        return remote(view, view, mp_send.at[i, n, c], rows_recv.at[q, nth(n), c], to)

    def wait_rows(n, q, c):
        landed(rows.at[q, nth(n), lines(c)], rows_recv.at[q, nth(n), c])

    def gather(n, c):
        if n > 0:
            wait_rows(n, mq, c)
        spread_copy(n, 0, c).start()
        spread_copy(n, 1, c).start()

    def pass_on(n, c):
        wait_rows(n, second, c)
        spread_copy(n, 2, c).start()

    def rows_of(q):
        return pl.ds(pl.multiple_of(q * eighth, eighth), eighth)

    def turn(begin, end):
        def step(i, carry):
            turned[:, rows_of(i)] = weights[rows_of(i), :].T
            return carry

        lax.fori_loop(begin, end, step, 0)

    def acc_copy(n):
        return remote(acc_out.at[way(n)], acc_in.at[n], acc_send.at[n], acc_recv.at[n], mate)

    def multiply(n, whose, sources, fresh):
        shard = nth(n)

        def step(j, carry):
            cols = pl.ds(pl.multiple_of(j * LANES, LANES), LANES)
            at = pl.ds(pl.multiple_of(whose * 2 * mine_w + j * LANES, LANES), LANES)
            total = None if fresh else acc[way(n), whose, :, cols]
            for q in sources:
                term = jnp.dot(
                    rows[q, shard], weights[rows_of(q), at], preferred_element_type=jnp.float32
                )
                total = term if total is None else total + term
            acc[way(n), whose, :, cols] = total
            return carry

        lax.fori_loop(0, 2 * mine_w // LANES, step, 0)

    def project(n):
        if n > 3:
            acc_copy(n - 3).wait_send()
        for c in chunks:
            wait_rows(n, first, c)
        for whose in (1, 0):
            multiply(n, whose, (mq, second, first), True)

    def finish(n):
        for c in chunks:
            wait_rows(n, across, c)
        multiply(n, 1, (across,), False)
        acc_out[way(n)] = acc[way(n), 1].astype(jnp.bfloat16)
        acc_copy(n).start()
        multiply(n, 0, (across,), False)

    scaling = HD ** (-0.5)
    position = lax.broadcasted_iota(jnp.int32, (source, query_v.shape[1]), 0)

    def grads_copy(n):
        return remote(
            row_grads.at[n, 0], row_grads.at[n, 1], grads_send.at[n], grads_recv.at[n], mate
        )

    def attend(n):
        shard = nth(n)
        if n > 0:
            landed(got_len.at[shard], len_recv.at[shard])
        landed(acc_in.at[n], acc_recv.at[n])
        visible = position < got_len[shard][0:1, :]
        for h in range(mine_w // HD):
            cols = slice(h * HD, (h + 1) * HD)
            wide = slice(mine_w + h * HD, mine_w + (h + 1) * HD)
            k = (acc[way(n), 0, :, cols] + acc_in[n, :, cols]).astype(jnp.bfloat16)
            v = (acc[way(n), 0, :, wide] + acc_in[n, :, wide]).astype(jnp.bfloat16)
            q = query_v[shard, :, cols]
            d = grad_v[shard, :, cols]
            scores = lax.dot_general(k, q, NT, preferred_element_type=jnp.float32) * scaling
            weight = jnp.where(visible, jnp.exp(scores), 0.0)
            probs = weight / jnp.sum(weight, axis=0, keepdims=True)
            grad_probs = lax.dot_general(v, d, NT, preferred_element_type=jnp.float32)
            deltas = jnp.sum(probs * grad_probs, axis=0, keepdims=True)
            grad_scores = (probs * (grad_probs - deltas) * scaling).astype(jnp.bfloat16)
            row_grads[n, 0, :, cols] = jnp.dot(
                grad_scores, q, preferred_element_type=jnp.float32
            ).astype(jnp.bfloat16)
            row_grads[n, 0, :, wide] = jnp.dot(
                probs.astype(jnp.bfloat16), d, preferred_element_type=jnp.float32
            ).astype(jnp.bfloat16)
        grads_copy(n).start()

    def part_copy(n, i, c):
        to = (ms, ml, second if i == 2 else first)
        return remote(
            part.at[i, n, lines(c)],
            inbox.at[i, n, lines(c)],
            part_send.at[i, n, c],
            part_recv.at[i, n, c],
            to,
        )

    def part_landed(n, i, c):
        landed(inbox.at[i, n, lines(c)], part_recv.at[i, n, c])
        return inbox[i, n, lines(c)].astype(jnp.float32)

    def project_back(n, q):
        at = rows_of(q)
        return jnp.dot(
            row_grads[n, 0], turned[0 : 2 * mine_w, at], preferred_element_type=jnp.float32
        ) + jnp.dot(
            row_grads[n, 1], turned[2 * mine_w :, at], preferred_element_type=jnp.float32
        )

    def send_back(n):
        landed(row_grads.at[n, 1], grads_recv.at[n])
        for i, q in enumerate((across, first)):
            part[i, n] = project_back(n, q).astype(jnp.bfloat16)
            for c in chunks:
                part_copy(n, i, c).start()

    def keep_back(n):
        own[1, way(n)] = project_back(n, second)
        own[0, way(n)] = project_back(n, mq)

    def sum_on(n, c):
        kept = own[1, way(n), lines(c)]
        part[2, n, lines(c)] = (kept + part_landed(n, 0, c)).astype(jnp.bfloat16)
        part_copy(n, 2, c).start()

    def back_copy(n, c):
        return remote(
            reduced.at[n, lines(c)],
            arrived.at[ml, lines(c)],
            back_send.at[n, c],
            back_recv.at[ml, c],
            (ms, nth(n), mq),
        )

    def give_back(n, c):
        total = own[0, way(n), lines(c)] + part_landed(n, 1, c)
        total = (total + part_landed(n, 2, c)).astype(jnp.bfloat16)
        if n == 0:
            arrived[ml, lines(c)] = total
        else:
            reduced[n, lines(c)] = total
            back_copy(n, c).start()

    inner = edge > 0

    def shift_rest(when):
        @pl.when(when)
        def _():
            for n in range(2, groups):
                shift(n)

    def share():
        for copy in share_copies():
            copy.start()

    rest = list(loads)

    def loaded():
        while rest:
            rest.pop(0).wait()

    def project_loaded(n):
        loaded()
        project(n)

    def turn_loaded(i):
        loaded()
        turn(i, i + 1)

    shared = list(enumerate(pairs))

    def attend_shared(n):
        while shared:
            i, (_, held) = shared.pop(0)
            landed(held.at[shards_there], share_recv.at[i])
        attend(n)

    steps = {
        "shift_near": lambda n: shift(1),
        "shift_inner": lambda n: shift_rest(inner),
        "shift_outer": lambda n: shift_rest(jnp.logical_not(inner)),
        "share": lambda n: share(),
        "turn": turn_loaded,
        "gather": gather,
        "pass_on": pass_on,
        "project": project_loaded,
        "finish": finish,
        "attend": attend_shared,
        "send_back": send_back,
        "keep_back": keep_back,
        "sum_on": sum_on,
        "give_back": give_back,
    }
    skip = groups - 4
    plan = [
        (name, n if name == "turn" or n == 0 else n + skip, *c) for name, n, *c in PLAN
    ]
    if skip > 0:
        lead = [step for step in plan if step[0] in LEAD]
        rest_of = [step for step in plan if step[0] not in LEAD]
        extra = []
        for n in range(1, skip + 1):
            for name in EXTRA:
                extra += [(name, n, c) for c in chunks] if name in PARTED else [(name, n)]
        plan = lead + extra + rest_of
    for name, n, *c in plan:
        steps[name](n, *c)

    for n in range(1, groups):
        g = nth(n)
        for c in chunks:
            landed(arrived.at[g, lines(c)], back_recv.at[g, c])
    for j in range(blocks):
        group = 0
        for c in range(languages):
            group = group + jnp.where(rank[c] == j, live[c] * group_of_lang[c], 0)
        out[0, j] = arrived[group]

    for copy in share_copies():
        copy.wait_send()
    for n in range(groups):
        if n > 0:
            for copy in shift_copies(n):
                copy.wait_send()
            for c in chunks:
                back_copy(n, c).wait_send()
        for i in range(3):
            for c in chunks:
                spread_copy(n, i, c).wait_send()
                part_copy(n, i, c).wait_send()
        if n == 0 or n > groups - 4:
            acc_copy(n).wait_send()
        grads_copy(n).wait_send()


def body(memory, queries, out_grad, key_weight, value_weight, lang_rows, group_of_lang, src_len):
    blocks, source, eighth = memory.shape[1:]
    width, heads_w = key_weight.shape[1:]
    sectors, groups = lax.axis_size("sect"), lax.axis_size("lang")
    quarters = lax.axis_size("mp")
    half, target = queries.shape[1:3]
    mine_w, depth = heads_w // sectors, width // sectors
    assert sectors == 2 and quarters == 4 and groups >= 2
    dims = (sectors, groups, quarters, half, blocks, source, eighth, width, heads_w)
    low, full = jnp.bfloat16, jnp.float32
    vmem = pl.BlockSpec(memory_space=pltpu.VMEM)
    smem = pl.BlockSpec(memory_space=pltpu.SMEM)
    hbm = pl.BlockSpec(memory_space=pl.ANY)
    dma = pltpu.SemaphoreType.DMA
    scratch = [
        pltpu.VMEM((depth, 2 * heads_w), low),
        pltpu.VMEM((2 * heads_w, depth), low),
        pltpu.VMEM(memory.shape, low),
        pltpu.VMEM((groups, target, mine_w), low),
        pltpu.VMEM((groups, target, mine_w), low),
        pltpu.VMEM((groups, source, eighth), low),
        pltpu.VMEM((groups, 8, target), jnp.int32),
        pltpu.VMEM((groups, 8, target), jnp.int32),
        pltpu.VMEM((quarters, groups, source, eighth), low),
        pltpu.VMEM((4, 2, source, 2 * mine_w), full),
        pltpu.VMEM((4, source, 2 * mine_w), low),
        pltpu.VMEM((groups, source, 2 * mine_w), low),
        pltpu.VMEM((groups, 2, source, 2 * mine_w), low),
        pltpu.VMEM((3, groups, source, eighth), low),
        pltpu.VMEM((2, 4, source, eighth), full),
        pltpu.VMEM((3, groups, source, eighth), low),
        pltpu.VMEM((groups, source, eighth), low),
        pltpu.VMEM((groups, source, eighth), low),
        dma((7,)),
        dma((2,)),
        dma((2,)),
        dma((groups, CHUNKS)),
        dma((groups,)),
        dma((groups,)),
        dma((quarters, groups, CHUNKS)),
        dma((3, groups, CHUNKS)),
        dma((groups,)),
        dma((groups,)),
        dma((groups,)),
        dma((groups,)),
        dma((3, groups, CHUNKS)),
        dma((3, groups, CHUNKS)),
        dma((groups, CHUNKS)),
        dma((groups, CHUNKS)),
    ]
    return pl.pallas_call(
        functools.partial(kernel, dims),
        out_shape=jax.ShapeDtypeStruct(memory.shape, memory.dtype),
        in_specs=[smem, smem, smem, hbm, hbm, hbm, hbm, hbm],
        out_specs=vmem,
        scratch_shapes=scratch,
        compiler_params=pltpu.CompilerParams(
            collective_id=0, has_side_effects=True, vmem_limit_bytes=67043328
        ),
    )(lang_rows, group_of_lang, src_len, memory, queries, out_grad, key_weight, value_weight)


def solution(mesh):
    in_specs = (
        P("lang", None, None, ("sect", "mp")),
        P("lang", "sect", None, "mp"),
        P("lang", "sect", None, "mp"),
        P("lang", None, "mp"),
        P("lang", None, "mp"),
        P("lang", None),
        P(),
        P("lang", None),
    )
    out_specs = P("lang", None, None, ("sect", "mp"))
    return jax.shard_map(body, mesh=mesh, in_specs=in_specs, out_specs=out_specs, check_vma=False)
```

```python
import functools

import jax
import jax.numpy as jnp
from jax import lax
from jax.experimental import pallas as pl
from jax.experimental.pallas import tpu as pltpu
from jax.sharding import PartitionSpec as P

HD = 128
LANES = 256
CHUNKS = 2
PLAN = (
    ("shift_near", 0),
    ("gather", 0, 0),
    ("gather", 0, 1),
    ("shift_inner", 0),
    ("share", 0),
    ("turn", 0),
    ("turn", 1),
    ("pass_on", 0, 0),
    ("pass_on", 0, 1),
    ("gather", 1, 0),
    ("gather", 1, 1),
    ("shift_outer", 0),
    ("turn", 2),
    ("turn", 3),
    ("project", 0),
    ("finish", 0),
    ("pass_on", 1, 0),
    ("gather", 2, 0),
    ("pass_on", 1, 1),
    ("gather", 2, 1),
    ("attend", 0),
    ("project", 1),
    ("finish", 1),
    ("pass_on", 2, 0),
    ("gather", 3, 0),
    ("pass_on", 2, 1),
    ("gather", 3, 1),
    ("attend", 1),
    ("send_back", 1),
    ("keep_back", 1),
    ("project", 2),
    ("finish", 2),
    ("pass_on", 3, 0),
    ("pass_on", 3, 1),
    ("sum_on", 1, 0),
    ("sum_on", 1, 1),
    ("attend", 2),
    ("send_back", 2),
    ("keep_back", 2),
    ("give_back", 1, 0),
    ("give_back", 1, 1),
    ("project", 3),
    ("finish", 3),
    ("sum_on", 2, 0),
    ("sum_on", 2, 1),
    ("attend", 3),
    ("send_back", 3),
    ("keep_back", 3),
    ("give_back", 2, 0),
    ("give_back", 2, 1),
    ("send_back", 0),
    ("keep_back", 0),
    ("sum_on", 3, 0),
    ("sum_on", 3, 1),
    ("give_back", 3, 0),
    ("give_back", 3, 1),
    ("sum_on", 0, 0),
    ("sum_on", 0, 1),
    ("give_back", 0, 0),
    ("give_back", 0, 1),
)
EXTRA = (
    "gather",
    "pass_on",
    "project",
    "finish",
    "attend",
    "send_back",
    "keep_back",
    "sum_on",
    "give_back",
)
PARTED = ("gather", "pass_on", "sum_on", "give_back")
LEAD = ("shift_near", "shift_inner", "shift_outer", "share", "turn")
MESH = pl.DeviceIdType.MESH
NT = (((1,), (1,)), ((), ()))


def kernel(
    dims,
    lang_rows,
    group_of_lang,
    src_len,
    memory_hbm,
    queries_hbm,
    grads_hbm,
    key_hbm,
    value_hbm,
    out,
    weights,
    turned,
    memory,
    query_v,
    grad_v,
    outgoing,
    out_len,
    got_len,
    rows,
    acc,
    acc_out,
    acc_in,
    row_grads,
    part,
    own,
    inbox,
    reduced,
    arrived,
    load_sem,
    share_send,
    share_recv,
    z_send,
    z_len_send,
    len_recv,
    rows_recv,
    mp_send,
    acc_send,
    acc_recv,
    grads_send,
    grads_recv,
    part_send,
    part_recv,
    back_send,
    back_recv,
):
    sectors, groups, quarters, half, blocks, source, eighth, width, heads_w = dims
    ms, ml, mq = lax.axis_index("sect"), lax.axis_index("lang"), lax.axis_index("mp")
    languages = lang_rows.shape[1]
    mate = (1 - ms, ml, mq)
    mine_w = heads_w // sectors
    depth = width // sectors

    near = mq + 1 - 2 * lax.rem(mq, 2)
    far = mq + 2 - 4 * lax.div(mq, 2)
    first = jnp.where(ms == 0, near, far)
    second = jnp.where(ms == 0, far, near)
    across = quarters - 1 - mq

    side = jnp.where(ml < groups - 1 - ml, 1, -1)
    edge = jnp.minimum(ml, groups - 1 - ml)

    def sent(n):
        close = (n + 1) // 2 if n % 2 else -(n // 2)
        return ml + side * jnp.where(n <= 2 * edge, close, n - edge)

    far_end = jnp.maximum(2 * edge, 1) + 1

    def nth(n):
        close = (n + 1) // 2 if n % 2 else -(n // 2)
        beyond = far_end + groups - 1 - n - edge
        return ml + side * jnp.where(n < far_end, jnp.where(n <= 2 * edge, close, n - edge), beyond)

    fetch = pltpu.make_async_copy(memory_hbm, memory, load_sem.at[0])
    fetch.start()
    barrier = pltpu.get_barrier_semaphore()
    peers = [(ms, nth(n), mq) for n in range(groups - 1, 0, -1)]
    peers += [(ms, ml, near), (ms, ml, far), mate]
    for peer in peers:
        pl.semaphore_signal(barrier, inc=1, device_id=peer, device_id_type=MESH)

    loads = []
    rows_here = pl.ds(pl.multiple_of(ms * depth, depth), depth)
    for i, (ref, owner) in enumerate(
        [(key_hbm, ms), (value_hbm, ms), (key_hbm, 1 - ms), (value_hbm, 1 - ms)]
    ):
        cols = pl.ds(pl.multiple_of(owner * mine_w, mine_w), mine_w)
        loads.append(
            pltpu.make_async_copy(
                ref.at[0, rows_here, cols],
                weights.at[:, pl.ds(i * mine_w, mine_w)],
                load_sem.at[1 + i],
            )
        )
    cols_here = pl.ds(pl.multiple_of(ms * mine_w, mine_w), mine_w)
    cols_there = pl.ds(pl.multiple_of((1 - ms) * mine_w, mine_w), mine_w)
    shards_here = pl.ds(ms * half, half)
    shards_there = pl.ds((1 - ms) * half, half)
    pairs = [(queries_hbm, query_v), (grads_hbm, grad_v)]
    for i, (ref, held) in enumerate(pairs):
        loads.append(
            pltpu.make_async_copy(
                ref.at[0, :, :, cols_here], held.at[shards_here], load_sem.at[5 + i]
            )
        )
    for load in loads:
        load.start()

    live, rank, count = [], [], 0
    for c in range(languages):
        live.append((lang_rows[0, c] > 0).astype(jnp.int32))
        rank.append(count)
        count = count + live[c]
    fetch.wait()
    for n in range(groups):
        g = sent(n)
        index, routed = 0, 0
        for c in range(languages):
            hit = jnp.where(group_of_lang[c] == g, live[c], 0)
            index = index + hit * rank[c]
            routed = routed + hit
        length = jnp.maximum(jnp.where(routed > 0, src_len[0, index], 1), 1)
        if n == 0:
            rows[mq, ml] = memory[0, index]
            got_len[ml] = jnp.full(out_len.shape[1:], length, jnp.int32)
        else:
            outgoing[n] = memory[0, index]
            out_len[n] = jnp.full(out_len.shape[1:], length, jnp.int32)

    pl.semaphore_wait(barrier, groups - 1 + 3)

    def way(n):
        return 0 if n == 0 else 1 + (n - 1) % 3

    def remote(src, dst, send, recv, to):
        return pltpu.make_async_remote_copy(
            src_ref=src,
            dst_ref=dst,
            send_sem=send,
            recv_sem=recv,
            device_id=to,
            device_id_type=MESH,
        )

    def landed(view, sem):
        pltpu.make_async_copy(view, view, sem).wait()

    size = source // CHUNKS
    chunks = range(CHUNKS)

    def lines(c):
        return pl.ds(c * size, size)

    def shift_copies(n):
        to = (ms, sent(n), mq)
        return [
            remote(
                outgoing.at[n, lines(c)],
                rows.at[mq, ml, lines(c)],
                z_send.at[n, c],
                rows_recv.at[mq, ml, c],
                to,
            )
            for c in chunks
        ] + [remote(out_len.at[n], got_len.at[ml], z_len_send.at[n], len_recv.at[ml], to)]

    def shift(n):
        for copy in shift_copies(n):
            copy.start()

    def share_copies():
        return [
            remote(
                ref.at[0, :, :, cols_there],
                held.at[shards_here],
                share_send.at[i],
                share_recv.at[i],
                mate,
            )
            for i, (ref, held) in enumerate(pairs)
        ]

    def spread_copy(n, i, c):
        to = (ms, ml, (first, second, first)[i])
        q = second if i == 2 else mq
        view = rows.at[q, nth(n), lines(c)]
        return remote(view, view, mp_send.at[i, n, c], rows_recv.at[q, nth(n), c], to)

    def wait_rows(n, q, c):
        landed(rows.at[q, nth(n), lines(c)], rows_recv.at[q, nth(n), c])

    def gather(n, c):
        if n > 0:
            wait_rows(n, mq, c)
        spread_copy(n, 0, c).start()
        spread_copy(n, 1, c).start()

    def pass_on(n, c):
        wait_rows(n, second, c)
        spread_copy(n, 2, c).start()

    def rows_of(q):
        return pl.ds(pl.multiple_of(q * eighth, eighth), eighth)

    def turn(begin, end):
        def step(i, carry):
            turned[:, rows_of(i)] = weights[rows_of(i), :].T
            return carry

        lax.fori_loop(begin, end, step, 0)

    def acc_copy(n):
        return remote(acc_out.at[way(n)], acc_in.at[n], acc_send.at[n], acc_recv.at[n], mate)

    def multiply(n, whose, sources, fresh):
        shard = nth(n)

        def step(j, carry):
            cols = pl.ds(pl.multiple_of(j * LANES, LANES), LANES)
            at = pl.ds(pl.multiple_of(whose * 2 * mine_w + j * LANES, LANES), LANES)
            total = None if fresh else acc[way(n), whose, :, cols]
            for q in sources:
                term = jnp.dot(
                    rows[q, shard], weights[rows_of(q), at], preferred_element_type=jnp.float32
                )
                total = term if total is None else total + term
            acc[way(n), whose, :, cols] = total
            return carry

        lax.fori_loop(0, 2 * mine_w // LANES, step, 0)

    def project(n):
        if n > 3:
            acc_copy(n - 3).wait_send()
        for c in chunks:
            wait_rows(n, first, c)
        for whose in (1, 0):
            multiply(n, whose, (mq, second, first), True)

    def finish(n):
        for c in chunks:
            wait_rows(n, across, c)
        multiply(n, 1, (across,), False)
        acc_out[way(n)] = acc[way(n), 1].astype(jnp.bfloat16)
        acc_copy(n).start()
        multiply(n, 0, (across,), False)

    scaling = HD ** (-0.5)
    position = lax.broadcasted_iota(jnp.int32, (source, query_v.shape[1]), 0)

    def grads_copy(n):
        return remote(
            row_grads.at[n, 0], row_grads.at[n, 1], grads_send.at[n], grads_recv.at[n], mate
        )

    def attend(n):
        shard = nth(n)
        if n > 0:
            landed(got_len.at[shard], len_recv.at[shard])
        landed(acc_in.at[n], acc_recv.at[n])
        visible = position < got_len[shard][0:1, :]
        for h in range(mine_w // HD):
            cols = slice(h * HD, (h + 1) * HD)
            wide = slice(mine_w + h * HD, mine_w + (h + 1) * HD)
            k = (acc[way(n), 0, :, cols] + acc_in[n, :, cols]).astype(jnp.bfloat16)
            v = (acc[way(n), 0, :, wide] + acc_in[n, :, wide]).astype(jnp.bfloat16)
            q = query_v[shard, :, cols]
            d = grad_v[shard, :, cols]
            scores = lax.dot_general(k, q, NT, preferred_element_type=jnp.float32) * scaling
            weight = jnp.where(visible, jnp.exp(scores), 0.0)
            probs = weight / jnp.sum(weight, axis=0, keepdims=True)
            grad_probs = lax.dot_general(v, d, NT, preferred_element_type=jnp.float32)
            deltas = jnp.sum(probs * grad_probs, axis=0, keepdims=True)
            grad_scores = (probs * (grad_probs - deltas) * scaling).astype(jnp.bfloat16)
            row_grads[n, 0, :, cols] = jnp.dot(
                grad_scores, q, preferred_element_type=jnp.float32
            ).astype(jnp.bfloat16)
            row_grads[n, 0, :, wide] = jnp.dot(
                probs.astype(jnp.bfloat16), d, preferred_element_type=jnp.float32
            ).astype(jnp.bfloat16)
        grads_copy(n).start()

    def part_copy(n, i, c):
        to = (ms, ml, second if i == 2 else first)
        return remote(
            part.at[i, n, lines(c)],
            inbox.at[i, n, lines(c)],
            part_send.at[i, n, c],
            part_recv.at[i, n, c],
            to,
        )

    def part_landed(n, i, c):
        landed(inbox.at[i, n, lines(c)], part_recv.at[i, n, c])
        return inbox[i, n, lines(c)].astype(jnp.float32)

    def project_back(n, q):
        at = rows_of(q)
        return jnp.dot(
            row_grads[n, 0], turned[0 : 2 * mine_w, at], preferred_element_type=jnp.float32
        ) + jnp.dot(
            row_grads[n, 1], turned[2 * mine_w :, at], preferred_element_type=jnp.float32
        )

    def send_back(n):
        landed(row_grads.at[n, 1], grads_recv.at[n])
        for i, q in enumerate((across, first)):
            part[i, n] = project_back(n, q).astype(jnp.bfloat16)
            for c in chunks:
                part_copy(n, i, c).start()

    def keep_back(n):
        own[1, way(n)] = project_back(n, second)
        own[0, way(n)] = project_back(n, mq)

    def sum_on(n, c):
        kept = own[1, way(n), lines(c)]
        part[2, n, lines(c)] = (kept + part_landed(n, 0, c)).astype(jnp.bfloat16)
        part_copy(n, 2, c).start()

    def back_copy(n, c):
        return remote(
            reduced.at[n, lines(c)],
            arrived.at[ml, lines(c)],
            back_send.at[n, c],
            back_recv.at[ml, c],
            (ms, nth(n), mq),
        )

    def give_back(n, c):
        total = own[0, way(n), lines(c)] + part_landed(n, 1, c)
        total = (total + part_landed(n, 2, c)).astype(jnp.bfloat16)
        if n == 0:
            arrived[ml, lines(c)] = total
        else:
            reduced[n, lines(c)] = total
            back_copy(n, c).start()

    inner = edge > 0

    def shift_rest(when):
        @pl.when(when)
        def _():
            for n in range(2, groups):
                shift(n)

    def share():
        for copy in share_copies():
            copy.start()

    rest = list(loads)

    def loaded():
        while rest:
            rest.pop(0).wait()

    def project_loaded(n):
        loaded()
        project(n)

    def turn_loaded(i):
        loaded()
        turn(i, i + 1)

    shared = list(enumerate(pairs))

    def attend_shared(n):
        while shared:
            i, (_, held) = shared.pop(0)
            landed(held.at[shards_there], share_recv.at[i])
        attend(n)

    steps = {
        "shift_near": lambda n: shift(1),
        "shift_inner": lambda n: shift_rest(inner),
        "shift_outer": lambda n: shift_rest(jnp.logical_not(inner)),
        "share": lambda n: share(),
        "turn": turn_loaded,
        "gather": gather,
        "pass_on": pass_on,
        "project": project_loaded,
        "finish": finish,
        "attend": attend_shared,
        "send_back": send_back,
        "keep_back": keep_back,
        "sum_on": sum_on,
        "give_back": give_back,
    }
    skip = groups - 4
    plan = [
        (name, n if name == "turn" or n == 0 else n + skip, *c) for name, n, *c in PLAN
    ]
    if skip > 0:
        lead = [step for step in plan if step[0] in LEAD]
        rest_of = [step for step in plan if step[0] not in LEAD]
        extra = []
        for n in range(1, skip + 1):
            for name in EXTRA:
                extra += [(name, n, c) for c in chunks] if name in PARTED else [(name, n)]
        plan = lead + extra + rest_of
    for name, n, *c in plan:
        steps[name](n, *c)

    for copy in share_copies():
        copy.wait_send()
    for n in range(groups):
        if n > 0:
            for copy in shift_copies(n):
                copy.wait_send()
        for i in range(3):
            for c in chunks:
                spread_copy(n, i, c).wait_send()
                part_copy(n, i, c).wait_send()
        if n == 0 or n > groups - 4:
            acc_copy(n).wait_send()
        grads_copy(n).wait_send()

    for n in range(1, groups):
        g = nth(n)
        for c in chunks:
            landed(arrived.at[g, lines(c)], back_recv.at[g, c])
    for j in range(blocks):
        group = 0
        for c in range(languages):
            group = group + jnp.where(rank[c] == j, live[c] * group_of_lang[c], 0)
        out[0, j] = arrived[group]

    for n in range(1, groups):
        for c in chunks:
            back_copy(n, c).wait_send()


def body(memory, queries, out_grad, key_weight, value_weight, lang_rows, group_of_lang, src_len):
    blocks, source, eighth = memory.shape[1:]
    width, heads_w = key_weight.shape[1:]
    sectors, groups = lax.axis_size("sect"), lax.axis_size("lang")
    quarters = lax.axis_size("mp")
    half, target = queries.shape[1:3]
    mine_w, depth = heads_w // sectors, width // sectors
    assert sectors == 2 and quarters == 4 and groups >= 2
    dims = (sectors, groups, quarters, half, blocks, source, eighth, width, heads_w)
    low, full = jnp.bfloat16, jnp.float32
    vmem = pl.BlockSpec(memory_space=pltpu.VMEM)
    smem = pl.BlockSpec(memory_space=pltpu.SMEM)
    hbm = pl.BlockSpec(memory_space=pl.ANY)
    dma = pltpu.SemaphoreType.DMA
    scratch = [
        pltpu.VMEM((depth, 2 * heads_w), low),
        pltpu.VMEM((2 * heads_w, depth), low),
        pltpu.VMEM(memory.shape, low),
        pltpu.VMEM((groups, target, mine_w), low),
        pltpu.VMEM((groups, target, mine_w), low),
        pltpu.VMEM((groups, source, eighth), low),
        pltpu.VMEM((groups, 8, target), jnp.int32),
        pltpu.VMEM((groups, 8, target), jnp.int32),
        pltpu.VMEM((quarters, groups, source, eighth), low),
        pltpu.VMEM((4, 2, source, 2 * mine_w), full),
        pltpu.VMEM((4, source, 2 * mine_w), low),
        pltpu.VMEM((groups, source, 2 * mine_w), low),
        pltpu.VMEM((groups, 2, source, 2 * mine_w), low),
        pltpu.VMEM((3, groups, source, eighth), low),
        pltpu.VMEM((2, 4, source, eighth), full),
        pltpu.VMEM((3, groups, source, eighth), low),
        pltpu.VMEM((groups, source, eighth), low),
        pltpu.VMEM((groups, source, eighth), low),
        dma((7,)),
        dma((2,)),
        dma((2,)),
        dma((groups, CHUNKS)),
        dma((groups,)),
        dma((groups,)),
        dma((quarters, groups, CHUNKS)),
        dma((3, groups, CHUNKS)),
        dma((groups,)),
        dma((groups,)),
        dma((groups,)),
        dma((groups,)),
        dma((3, groups, CHUNKS)),
        dma((3, groups, CHUNKS)),
        dma((groups, CHUNKS)),
        dma((groups, CHUNKS)),
    ]
    return pl.pallas_call(
        functools.partial(kernel, dims),
        out_shape=jax.ShapeDtypeStruct(memory.shape, memory.dtype),
        in_specs=[smem, smem, smem, hbm, hbm, hbm, hbm, hbm],
        out_specs=vmem,
        scratch_shapes=scratch,
        compiler_params=pltpu.CompilerParams(
            collective_id=0, has_side_effects=True, vmem_limit_bytes=67043328
        ),
    )(lang_rows, group_of_lang, src_len, memory, queries, out_grad, key_weight, value_weight)


def solution(mesh):
    in_specs = (
        P("lang", None, None, ("sect", "mp")),
        P("lang", "sect", None, "mp"),
        P("lang", "sect", None, "mp"),
        P("lang", None, "mp"),
        P("lang", None, "mp"),
        P("lang", None),
        P(),
        P("lang", None),
    )
    out_specs = P("lang", None, None, ("sect", "mp"))
    return jax.shard_map(body, mesh=mesh, in_specs=in_specs, out_specs=out_specs, check_vma=False)
```
